32 devices in a mesh: obj: 4 (over z), dp: 4 (over x, core), tp: 2 (over y).
Axes of the slice: x: 2, y: 2, z: 4, core: 2. Of those that a mesh axis runs over, the one named last changes fastest.
Arguments:
- hidden_in: bfloat16 [16, 1024, 2048], P(('obj', 'dp'), 'tp'), may hold values from -6 to 6
- cotangent: bfloat16 [16, 1024, 2048], P(('obj', 'dp'), 'tp'), may hold values from -6 to 6
- loss_mask: int32 [16, 1024], P(('obj', 'dp'), 'tp'), may hold values from 0 to 1, as said below
- prefix_len: int32 [16], P(('obj', 'dp')), may hold values from 256 to 1024, as said below
- w_qkv: bfloat16 [2048, 3, 2048], P(None, None, 'tp'), may hold values from -0.1875 to 0.1875
- w_out: bfloat16 [2048, 2048], P('tp'), may hold values from -1 to 1
- gain_one: float32 [2048], replicated, may hold values from 0.5 to 1.5
- bias_one: float32 [2048], replicated, may hold values from -3 to 3
- w_gate_up: bfloat16 [2048, 2, 5632], P(None, None, 'tp'), may hold values from -0.125 to 0.125
- w_down: bfloat16 [5632, 2048], P('tp'), may hold values from -0.625 to 0.625
- gain_two: float32 [2048], replicated, may hold values from 0.5 to 1.5
- bias_two: float32 [2048], replicated, may hold values from -3 to 3
Outputs:
- outputs: bfloat16 [16, 1024, 2048], P(('obj', 'dp'), 'tp')
- input_grad: float32 [16, 1024, 2048], P(('obj', 'dp'), 'tp')
- grad_qkv: float32 [2048, 3, 2048], P(None, None, 'tp')
- grad_out: float32 [2048, 2048], P('tp')
- grad_gain_one: float32 [2048], P('tp')
- grad_bias_one: float32 [2048], P('tp')
- grad_gate_up: float32 [2048, 2, 5632], P(None, None, 'tp')
- grad_down: float32 [5632, 2048], P('tp')
- grad_gain_two: float32 [2048], P('tp')
- grad_bias_two: float32 [2048], P('tp')
The draws below stay inside these ranges and needn't reach their ends.
Inputs may be any that keep to these rules, and one draw needn't show every extreme that they name: `loss_mask`: group 0 holds MLM chains, whose ones are masked positions (always including the last token of a live chain); the other groups hold GLM chains, whose ones are the tokens at or after prefix_len. Padding chains, the last slots of groups 0 to 2, are all zero. Every group has a one. `prefix_len`: every chain of group 0 has prefix 1024 and attends both ways; GLM chains have prefixes from 256 to 768.
All inputs are finite; a program needn't handle non-finite values.
Results may differ from the reference program's by a relative error of at most 0.017.
The reference program's roundings to bfloat16 on the way count: a program that leaves them out, or rounds other values in their place, can miss the bound.
Values may be sent and summed in bfloat16 or wider, within the bound.
A program may use at most 448 MiB of HBM per device.

```python
import jax
import jax.numpy as jnp
from jax import lax

D = 2048
HEADS = 16
HEAD_DIM = 128
FF = 5632
LEN = 1024
SLOTS_G = 4
SLOTS = 16
N_OBJ = 4


def plan_chains(key):
    prefix_key, mask_key = jax.random.split(jax.random.fold_in(key, 11))
    slot_ids = jnp.arange(SLOTS, dtype=jnp.int32)
    group_ids = slot_ids // SLOTS_G
    within = slot_ids % SLOTS_G
    padding = jnp.where(group_ids == 0, 2, jnp.where(group_ids < 3, 1, 0))
    live_slot = within < SLOTS_G - padding
    glm_prefix = jax.random.randint(prefix_key, (SLOTS,), LEN // 4, 3 * LEN // 4 + 1, dtype=jnp.int32)
    prefix_len = jnp.where(group_ids == 0, LEN, glm_prefix).astype(jnp.int32)
    positions = jnp.arange(LEN, dtype=jnp.int32)
    rising = 80 + 300 * (within[:, None] * LEN + positions[None, :]) // (SLOTS_G * LEN)
    lottery = jax.random.randint(mask_key, (SLOTS, LEN), 0, 1000, dtype=jnp.int32)
    masked = (lottery < rising) | (positions[None, :] == LEN - 1)
    span_marks = positions[None, :] >= prefix_len[:, None]
    marked = jnp.where((group_ids == 0)[:, None], masked, span_marks) & live_slot[:, None]
    return (prefix_len, marked.astype(jnp.int32))


def draw_loss_mask(key, part):
    return plan_chains(key)[1]


def draw_prefix_len(key, part):
    return plan_chains(key)[0]


def level_of(rng, extent, pieces, low, top_value):
    loudness, own = 1.0, jax.random.fold_in(rng, 6)
    for axis_at, shards_of in pieces:
        draws = jnp.exp(jax.random.uniform(jax.random.fold_in(own, axis_at), (shards_of,), jnp.float32, low / len(pieces), top_value / len(pieces)))
        loudness = loudness * jnp.repeat(draws, extent[axis_at] // shards_of).reshape([-1 if axis == axis_at else 1 for axis in range(len(extent))])
    return loudness


def scatter_about(rng, dims, deviation, most, shards=(), held_as=jnp.bfloat16):
    entries = jax.random.normal(rng, dims, jnp.float32) * deviation
    if len(shards) > 0:
        entries = level_of(rng, dims, shards, -0.22, 0.18) * entries
    return jnp.clip(entries, min=-most, max=most).astype(held_as)


def setup_inputs(seed: int = 0) -> dict:
    keys = jax.random.split(jax.random.key(seed), 13)
    return {
        "hidden_in": scatter_about(keys[0], (SLOTS, LEN, D), 1.0, 6.0, ((0, 16), (1, 2))),
        "cotangent": scatter_about(keys[1], (SLOTS, LEN, D), 1.0, 6.0, ((0, 16), (1, 2))),
        "loss_mask": draw_loss_mask(jax.random.fold_in(keys[12], 71), 0),
        "prefix_len": draw_prefix_len(jax.random.fold_in(keys[12], 71), 0),
        "w_qkv": scatter_about(keys[4], (D, 3, D), (1.5 / D ** 0.5), 0.1875, ((2, 2),)),
        "w_out": scatter_about(keys[5], (D, D), (8.0 / D ** 0.5), 1.0, ((0, 2),)),
        "gain_one": jnp.clip(1.0 + 0.1 * jax.random.normal(keys[6], (D,), jnp.float32), 0.5, 1.5),
        "bias_one": scatter_about(keys[7], (D,), 0.5, 3.0, (), jnp.float32),
        "w_gate_up": scatter_about(keys[8], (D, 2, FF), D ** -0.5, 0.125, ((2, 2),)),
        "w_down": scatter_about(keys[9], (FF, D), (8.0 / FF ** 0.5), 0.625, ((0, 2),)),
        "gain_two": jnp.clip(1.0 + 0.1 * jax.random.normal(keys[10], (D,), jnp.float32), 0.5, 1.5),
        "bias_two": scatter_about(keys[11], (D,), 0.5, 3.0, (), jnp.float32),
    }


DEEP_ALPHA = 48.0 ** 0.5
NORM_EPS = 1e-05
MASKED_SCORE = -1e+30
HIGHEST = lax.Precision.HIGHEST

@jax.custom_vjp
def low(v):
    return lax.optimization_barrier(v.astype(jnp.bfloat16)).astype(jnp.float32)

@jax.custom_vjp
def low_back(v):
    return v

def low_keep(v):
    return (low(v), None)

def low_pass(kept, grad):
    return (grad,)

def back_keep(v):
    return (v, None)

def back_low(kept, grad):
    return (low(grad),)
low.defvjp(low_keep, low_pass)
low_back.defvjp(back_keep, back_low)

def layer_norm(rows_in, norm_gain, norm_bias):
    row_mean = lax.optimization_barrier(jnp.mean(rows_in, axis=-1, keepdims=True))
    centred = rows_in - row_mean
    variance = lax.optimization_barrier(jnp.mean(centred * centred, axis=-1, keepdims=True))
    return centred * lax.rsqrt(variance + NORM_EPS) * norm_gain + norm_bias

def rotate(vectors, positions):
    half_dim = vectors.shape[-1] // 2
    frequency = 10000.0 ** (-jnp.arange(half_dim).astype(positions.dtype) / half_dim)
    angles = positions[:, None] * frequency[None, :]
    cos_vals = jnp.cos(angles)[:, None, :]
    sin_vals = jnp.sin(angles)[:, None, :]
    first_half = vectors[..., :half_dim]
    second_half = vectors[..., half_dim:]
    return jnp.concatenate([first_half * cos_vals - second_half * sin_vals, second_half * cos_vals + first_half * sin_vals], axis=-1)

def chain_layer(weights, chain_pair):
    chain_in, prefix = chain_pair
    w_qkv, w_out, gain_one, bias_one, w_gate_up, w_down, gain_two, bias_two = weights
    seq_len = chain_in.shape[0]
    proj_qkv = low_back(jnp.einsum('td,dke->tke', chain_in, w_qkv, precision=HIGHEST))
    head_shape = (seq_len, HEADS, HEAD_DIM)
    positions = jnp.arange(seq_len).astype(chain_in.dtype)
    queries = low(rotate(proj_qkv[:, 0].reshape(head_shape), positions))
    key_rows = low(rotate(proj_qkv[:, 1].reshape(head_shape), positions))
    values = low(proj_qkv[:, 2].reshape(head_shape))
    scores = low_back(jnp.einsum('qhe,khe->hqk', queries, key_rows, precision=HIGHEST) * HEAD_DIM ** (-0.5))
    token_ids = jnp.arange(seq_len, dtype=jnp.int32)
    allowed = (token_ids[None, :] < prefix) | (token_ids[None, :] <= token_ids[:, None])
    attn_probs = low(jax.nn.softmax(jnp.where(allowed[None], scores, MASKED_SCORE), axis=-1))
    mixed = jnp.einsum('hqk,khe->qhe', attn_probs, values, precision=HIGHEST).reshape(seq_len, HEADS * HEAD_DIM)
    mixed = low(low_back(mixed))
    attn_out = low_back(jnp.dot(mixed, w_out, precision=HIGHEST))
    h_one = layer_norm(DEEP_ALPHA * chain_in + attn_out, gain_one, bias_one)
    gate_up = low_back(jnp.einsum('td,dke->tke', low(h_one), w_gate_up, precision=HIGHEST))
    hidden = low(jax.nn.gelu(gate_up[:, 0], approximate=False) * gate_up[:, 1])
    ffn_out = low_back(jnp.dot(hidden, w_down, precision=HIGHEST))
    return layer_norm(DEEP_ALPHA * h_one + ffn_out, gain_two, bias_two)

def reference(hidden_in, cotangent, loss_mask, prefix_len, w_qkv, w_out, gain_one, bias_one, w_gate_up, w_down, gain_two, bias_two):
    weights = tuple((array_in.astype(jnp.float32) for array_in in (w_qkv, w_out, gain_one, bias_one, w_gate_up, w_down, gain_two, bias_two)))
    inputs = hidden_in.astype(jnp.float32)
    single = jax.checkpoint(chain_layer)

    def forward(weights, inputs):
        return lax.map(lambda chain_pair: single(weights, chain_pair), (inputs, prefix_len))
    outputs, pullback = jax.vjp(forward, weights, inputs)
    mask_vals = loss_mask.astype(jnp.float32)
    counts = lax.optimization_barrier(jnp.sum(mask_vals.reshape(N_OBJ, -1), axis=1))
    slot_scale = jnp.repeat(LEN / counts, SLOTS // N_OBJ)
    grad_y = cotangent.astype(jnp.float32) * (mask_vals * slot_scale[:, None])[..., None]
    weight_grads, input_grad = pullback(grad_y)
    grad_qkv, grad_out, grad_gain_one, grad_bias_one, grad_gate_up, grad_down, grad_gain_two, grad_bias_two = weight_grads
    return (outputs.astype(jnp.bfloat16), input_grad, grad_qkv, grad_out, grad_gain_one, grad_bias_one, grad_gate_up, grad_down, grad_gain_two, grad_bias_two)
```

```python
import functools

import jax
import jax.numpy as jnp
from jax import lax
from jax.experimental import pallas as pl
from jax.experimental.pallas import tpu as pltpu
from jax.sharding import PartitionSpec as P

HEAD_DIM = 128
DEEP_ALPHA = 48.0**0.5
NORM_EPS = 1e-05
MASKED_SCORE = -1e30
F32 = jnp.float32
BF16 = jnp.bfloat16
VMEM_BYTES = 60 * 1024 * 1024


def rotated(block, cos_ref, sin_ref, sign):
    half = block.shape[-1] // 2
    return block * cos_ref[...] + sign * (pltpu.roll(block, half, 1) * sin_ref[...])


def row_limits(info_ref, start, rows, seq_len):
    row_ids = lax.broadcasted_iota(jnp.int32, (1, rows), 1) + start + info_ref[0]
    row_ids = jnp.where(row_ids >= seq_len, row_ids - seq_len, row_ids)
    return jnp.maximum(row_ids, info_ref[1] - 1)


def key_ids(info_ref, seq_len):
    ids = lax.broadcasted_iota(jnp.int32, (seq_len, 1), 0) + info_ref[0]
    return jnp.where(ids >= seq_len, ids - seq_len, ids)


def attend_kernel(
    block_rows, info_ref, own_ref, other_ref, cos_ref, sin_ref, mixed_ref, qkv_ref
):
    share_len = own_ref.shape[1]
    seq_len = mixed_ref.shape[0]
    scale = HEAD_DIM**-0.5
    for part in range(3):
        block = jnp.concatenate([own_ref[part], other_ref[part]], axis=0)
        if part < 2:
            block = rotated(block, cos_ref, sin_ref, 1.0)
        qkv_ref[part] = block.astype(BF16)
    keys = qkv_ref[1]
    values = qkv_ref[2]
    ids = key_ids(info_ref, seq_len)
    for start in range(0, seq_len, block_rows):
        queries = qkv_ref[0, start : start + block_rows, :]
        scores = (
            lax.dot_general(keys, queries, (((1,), (1,)), ((), ())), preferred_element_type=F32)
            * scale
        )
        limits = row_limits(info_ref, start, block_rows, seq_len)
        scores = jnp.where(ids <= limits, scores, MASKED_SCORE)
        row_max = jnp.max(scores, axis=0, keepdims=True)
        weights = jnp.exp(scores - row_max)
        total = jnp.sum(weights, axis=0, keepdims=True)
        probs = (weights * (1.0 / total)).astype(BF16)
        mixed = lax.dot_general(
            probs, values, (((0,), (0,)), ((), ())), preferred_element_type=F32
        )
        mixed_ref[start : start + block_rows, :] = mixed.astype(BF16)


def attend_back_kernel(
    block_rows, info_ref, qkv_ref, grad_ref, cos_ref, sin_ref, out_ref, d_key_ref, d_value_ref
):
    seq_len = grad_ref.shape[0]
    scale = HEAD_DIM**-0.5
    keys = qkv_ref[1]
    values = qkv_ref[2]
    ids = key_ids(info_ref, seq_len)
    for start in range(0, seq_len, block_rows):
        rows = slice(start, start + block_rows)
        queries = qkv_ref[0, rows, :]
        grads = grad_ref[rows, :]
        scores = (
            lax.dot_general(keys, queries, (((1,), (1,)), ((), ())), preferred_element_type=F32)
            * scale
        )
        limits = row_limits(info_ref, start, block_rows, seq_len)
        scores = jnp.where(ids <= limits, scores, MASKED_SCORE)
        row_max = jnp.max(scores, axis=0, keepdims=True)
        weights = jnp.exp(scores - row_max)
        total = jnp.sum(weights, axis=0, keepdims=True)
        probs = weights * (1.0 / total)
        d_probs = lax.dot_general(
            values, grads, (((1,), (1,)), ((), ())), preferred_element_type=F32
        )
        delta = jnp.sum(probs * d_probs, axis=0, keepdims=True)
        d_scores = (probs * (d_probs - delta)).astype(BF16)
        d_value = jnp.dot(probs.astype(BF16), grads, preferred_element_type=F32)
        d_key = jnp.dot(d_scores, queries, preferred_element_type=F32)
        if start == 0:
            d_value_ref[...] = d_value
            d_key_ref[...] = d_key
        else:
            d_value_ref[...] += d_value
            d_key_ref[...] += d_key
        d_query = (
            lax.dot_general(d_scores, keys, (((0,), (0,)), ((), ())), preferred_element_type=F32)
            * scale
        )
        d_query = d_query * cos_ref[rows, :] - (
            pltpu.roll(d_query, HEAD_DIM // 2, 1) * sin_ref[rows, :]
        )
        out_ref[0, rows, :] = d_query.astype(BF16)
    d_key = d_key_ref[...] * scale
    out_ref[1] = rotated(d_key, cos_ref, sin_ref, -1.0).astype(BF16)
    out_ref[2] = d_value_ref[...].astype(BF16)


def attend(info, own, other, cos_vals, sin_vals):
    share_len, local_width = own.shape[1:]
    seq_len = share_len + other.shape[1]
    heads = local_width // HEAD_DIM
    table = pl.BlockSpec((seq_len, HEAD_DIM), lambda h, info: (0, 0))
    return pl.pallas_call(
        functools.partial(attend_kernel, min(256, seq_len)),
        grid_spec=pltpu.PrefetchScalarGridSpec(
            num_scalar_prefetch=1,
            grid=(heads,),
            in_specs=[
                pl.BlockSpec((3, share_len, HEAD_DIM), lambda h, info: (0, 0, h)),
                pl.BlockSpec((3, seq_len - share_len, HEAD_DIM), lambda h, info: (0, 0, h)),
                table,
                table,
            ],
            out_specs=[
                pl.BlockSpec((seq_len, HEAD_DIM), lambda h, info: (0, h)),
                pl.BlockSpec((3, seq_len, HEAD_DIM), lambda h, info: (0, 0, h)),
            ],
        ),
        out_shape=[
            jax.ShapeDtypeStruct((seq_len, local_width), BF16),
            jax.ShapeDtypeStruct((3, seq_len, local_width), BF16),
        ],
        compiler_params=pltpu.CompilerParams(vmem_limit_bytes=VMEM_BYTES),
        cost_estimate=pl.CostEstimate(
            flops=8 * seq_len * seq_len * local_width,
            bytes_accessed=seq_len * local_width * 20,
            transcendentals=seq_len * seq_len * heads,
        ),
        name="attend",
    )(info, own, other, cos_vals, sin_vals)


def attend_back(info, qkv, grads, cos_vals, sin_vals):
    seq_len, local_width = grads.shape
    heads = local_width // HEAD_DIM
    table = pl.BlockSpec((seq_len, HEAD_DIM), lambda h, info: (0, 0))
    return pl.pallas_call(
        functools.partial(attend_back_kernel, min(256, seq_len)),
        grid_spec=pltpu.PrefetchScalarGridSpec(
            num_scalar_prefetch=1,
            grid=(heads,),
            in_specs=[
                pl.BlockSpec((3, seq_len, HEAD_DIM), lambda h, info: (0, 0, h)),
                pl.BlockSpec((seq_len, HEAD_DIM), lambda h, info: (0, h)),
                table,
                table,
            ],
            out_specs=pl.BlockSpec((3, seq_len, HEAD_DIM), lambda h, info: (0, 0, h)),
            scratch_shapes=[
                pltpu.VMEM((seq_len, HEAD_DIM), F32),
                pltpu.VMEM((seq_len, HEAD_DIM), F32),
            ],
        ),
        out_shape=jax.ShapeDtypeStruct((3, seq_len, local_width), BF16),
        compiler_params=pltpu.CompilerParams(vmem_limit_bytes=VMEM_BYTES),
        cost_estimate=pl.CostEstimate(
            flops=20 * seq_len * seq_len * local_width,
            bytes_accessed=seq_len * local_width * 14,
            transcendentals=seq_len * seq_len * heads,
        ),
        name="attend_back",
    )(info, qkv, grads, cos_vals, sin_vals)


def gather_rows(own):
    size = lax.axis_size("tp")
    if size == 2:
        return lax.ppermute(own, "tp", [(0, 1), (1, 0)])
    share = own.shape[0]
    whole = lax.all_gather(own, "tp", axis=0, tiled=True)
    start = (lax.axis_index("tp") + 1) * share
    return lax.dynamic_slice_in_dim(
        jnp.concatenate([whole, whole], axis=0), start, (size - 1) * share, 0
    )


def scatter_rows(own_part, send_part):
    size = lax.axis_size("tp")
    if size == 2:
        return own_part + lax.ppermute(send_part, "tp", [(0, 1), (1, 0)]).astype(F32)
    share = own_part.shape[0]
    ring = jnp.concatenate([own_part.astype(BF16), send_part] * 2, axis=0)
    start = (size - lax.axis_index("tp")) * share
    whole = lax.dynamic_slice_in_dim(ring, start, size * share, 0)
    return lax.psum_scatter(whole.astype(F32), "tp", scatter_dimension=0, tiled=True)


def all_sum(value, axes):
    for axis in axes:
        size = lax.axis_size(axis)
        step = 1
        while step < size:
            value = value + lax.ppermute(value, axis, [(i, i ^ step) for i in range(size)])
            step *= 2
    return value


CORE_SWAP = [(0, 1), (1, 0), (2, 3), (3, 2)]
X_SWAP = [(0, 2), (2, 0), (1, 3), (3, 1)]
INWARD = [(0, 1), (3, 2)]
MIDDLE = [(1, 2), (2, 1)]
OUTWARD = [(1, 0), (2, 3)]


def reduce_quarters(make):
    dp_index = lax.axis_index("dp")
    obj_index = lax.axis_index("obj")
    x_bit, core_bit = dp_index // 2, dp_index % 2

    def quarter(x_same, core_same):
        x_at = x_bit if x_same else 1 - x_bit
        core_at = core_bit if core_same else 1 - core_bit
        return 2 * x_at + core_at

    give_far = make(quarter(False, False)).astype(BF16)
    give_near = make(quarter(True, False)).astype(BF16)
    got_far = lax.ppermute(give_far, "dp", CORE_SWAP)
    got_near = lax.ppermute(give_near, "dp", CORE_SWAP)
    far = (make(quarter(False, True)) + got_far.astype(F32)).astype(BF16)
    near = make(quarter(True, True)) + got_near.astype(F32)
    near = near + lax.ppermute(far, "dp", X_SWAP).astype(F32)
    near_low = near.astype(BF16)
    side = (near + lax.ppermute(near_low, "obj", INWARD).astype(F32)).astype(BF16)
    both = side + lax.ppermute(side, "obj", MIDDLE)
    in_middle = (obj_index == 1) | (obj_index == 2)
    mine = jnp.where(in_middle, both, lax.ppermute(both, "obj", OUTWARD))
    across = lax.ppermute(mine, "dp", X_SWAP)
    return (
        mine,
        across,
        lax.ppermute(mine, "dp", CORE_SWAP),
        lax.ppermute(across, "dp", CORE_SWAP),
    )


def in_order(quarters, axis):
    mine, across, mine_c, across_c = quarters
    dp_index = lax.axis_index("dp")
    x_is0 = dp_index // 2 == 0
    core_is0 = dp_index % 2 == 0
    c0_near, c1_near = jnp.where(core_is0, mine, mine_c), jnp.where(core_is0, mine_c, mine)
    c0_far, c1_far = jnp.where(core_is0, across, across_c), jnp.where(core_is0, across_c, across)
    return jnp.concatenate(
        [
            jnp.where(x_is0, c0_near, c0_far),
            jnp.where(x_is0, c1_near, c1_far),
            jnp.where(x_is0, c0_far, c0_near),
            jnp.where(x_is0, c1_far, c1_near),
        ],
        axis=axis,
    ).astype(F32)


def columns(array, index, count=4):
    width = array.shape[-1] // count
    return lax.dynamic_slice_in_dim(array, index * width, width, array.ndim - 1)


def token_sum(left, right):
    return lax.dot_general(left, right, (((0,), (0,)), ((), ())), preferred_element_type=F32)


def norm_stats(rows):
    mean = jnp.mean(rows, axis=-1, keepdims=True)
    centred = rows - mean
    scale = lax.rsqrt(jnp.mean(centred * centred, axis=-1, keepdims=True) + NORM_EPS)
    return centred * scale, scale


def norm_back(grads, zhat, scale, gain):
    q = grads * gain
    d_rows = scale * (
        q - jnp.mean(q, axis=-1, keepdims=True) - zhat * jnp.mean(q * zhat, axis=-1, keepdims=True)
    )
    return d_rows, jnp.sum(grads * zhat, axis=0), jnp.sum(grads, axis=0)


def body(
    hidden_in,
    cotangent,
    loss_mask,
    prefix_len,
    w_qkv,
    w_out,
    gain_one,
    bias_one,
    w_gate_up,
    w_down,
    gain_two,
    bias_two,
):
    tp_index = lax.axis_index("tp")
    share_len, width = hidden_in.shape[1:]
    seq_len = share_len * lax.axis_size("tp")
    local_ff = w_down.shape[0]
    mask_vals = loss_mask[0].astype(F32)
    total_count = all_sum(jnp.full((8, 128), jnp.sum(mask_vals)), ("dp", "tp"))[0, 0]

    positions = (tp_index * share_len + jnp.arange(seq_len, dtype=jnp.int32)) % seq_len
    half = HEAD_DIM // 2
    frequency = 10000.0 ** (-jnp.arange(half).astype(F32) / half)
    angles = positions.astype(F32)[:, None] * frequency[None, :]
    cos_half, sin_half = jnp.cos(angles), jnp.sin(angles)
    cos_vals = jnp.concatenate([cos_half, cos_half], axis=1)
    sin_vals = jnp.concatenate([-sin_half, sin_half], axis=1)
    info = jnp.stack([tp_index * share_len, prefix_len[0]]).astype(jnp.int32)

    def project(rows):
        return jnp.einsum("td,dke->kte", rows, w_qkv, preferred_element_type=F32)

    x_own = hidden_in[0]
    x_other = gather_rows(x_own)
    mixed, qkv = attend(info, project(x_own), project(x_other), cos_vals, sin_vals)
    mixed_own, mixed_other = mixed[:share_len], mixed[share_len:]
    out_send = jnp.dot(mixed_other, w_out, preferred_element_type=F32).astype(BF16)
    out_own = jnp.dot(mixed_own, w_out, preferred_element_type=F32)
    z_one = DEEP_ALPHA * x_own.astype(F32) + scatter_rows(out_own, out_send)
    zhat_one, scale_one = norm_stats(z_one)
    h_one = zhat_one * gain_one + bias_one
    h_own = h_one.astype(BF16)
    h_other = gather_rows(h_own)

    def feed(rows):
        gate_up = jnp.einsum("td,dke->tke", rows, w_gate_up, preferred_element_type=F32)
        gate, up = gate_up[:, 0], gate_up[:, 1]
        phi = 0.5 * (1.0 + lax.erf(gate * (0.5**0.5)))
        density = jnp.exp(-0.5 * gate * gate) * (0.5 / jnp.pi) ** 0.5
        act = gate * phi
        return lax.optimization_barrier(
            ((act * up).astype(BF16), up * (phi + gate * density), act)
        )

    hidden_own, slope_own, act_own = feed(h_own)
    hidden_other, slope_other, act_other = feed(h_other)
    ffn_send = jnp.dot(hidden_other, w_down, preferred_element_type=F32).astype(BF16)
    ffn_own = jnp.dot(hidden_own, w_down, preferred_element_type=F32)
    z_two = DEEP_ALPHA * h_one + scatter_rows(ffn_own, ffn_send)
    zhat_two, scale_two = norm_stats(z_two)
    outputs = (zhat_two * gain_two + bias_two).astype(BF16)
    grad_y = cotangent[0].astype(F32) * (mask_vals * (seq_len / total_count))[:, None]
    d_z_two, d_gain_two, d_bias_two = norm_back(grad_y, zhat_two, scale_two, gain_two)

    d_ffn_own = d_z_two.astype(BF16)
    d_ffn_other = gather_rows(d_ffn_own)
    hidden = jnp.concatenate([hidden_own, hidden_other], axis=0)
    d_ffn = jnp.concatenate([d_ffn_own, d_ffn_other], axis=0)

    def feed_back(d_rows, slope, act):
        d_hidden = lax.dot_general(
            d_rows, w_down, (((1,), (1,)), ((), ())), preferred_element_type=F32
        )
        return jnp.stack([d_hidden * slope, d_hidden * act], axis=0).astype(BF16)

    grad_down = reduce_quarters(lambda q: token_sum(hidden, columns(d_ffn, q)))
    d_gu_own = feed_back(d_ffn_own, slope_own, act_own)
    d_gu_other = feed_back(d_ffn_other, slope_other, act_other)
    d_gu = jnp.concatenate([d_gu_own, d_gu_other], axis=1)
    h_rows = jnp.concatenate([h_own, h_other], axis=0)
    grad_gate_up = [
        reduce_quarters(lambda q, k=k: token_sum(columns(h_rows, q), d_gu[k])) for k in range(2)
    ]

    def feed_rows(d_gate_up):
        return jnp.einsum("kte,dke->td", d_gate_up, w_gate_up, preferred_element_type=F32)

    d_h_send = feed_rows(d_gu_other).astype(BF16)
    d_h = scatter_rows(feed_rows(d_gu_own), d_h_send)
    d_z_one, d_gain_one, d_bias_one = norm_back(
        DEEP_ALPHA * d_z_two + d_h, zhat_one, scale_one, gain_one
    )
    d_attn_own = d_z_one.astype(BF16)
    d_attn_other = gather_rows(d_attn_own)
    d_attn = jnp.concatenate([d_attn_own, d_attn_other], axis=0)
    grad_out = reduce_quarters(lambda q: token_sum(mixed, columns(d_attn, q)))

    def unmix(d_rows):
        return lax.dot_general(
            d_rows, w_out, (((1,), (1,)), ((), ())), preferred_element_type=F32
        ).astype(BF16)

    d_mixed = jnp.concatenate([unmix(d_attn_own), unmix(d_attn_other)], axis=0)
    d_qkv = attend_back(info, qkv, d_mixed, cos_vals, sin_vals)
    x_rows = jnp.concatenate([x_own, x_other], axis=0)
    grad_qkv = [
        reduce_quarters(lambda q, k=k: token_sum(columns(x_rows, q), d_qkv[k])) for k in range(3)
    ]

    def unproject(d_rows):
        return jnp.einsum("kte,dke->td", d_rows, w_qkv, preferred_element_type=F32)

    d_x_send = unproject(d_qkv[:, share_len:]).astype(BF16)
    d_x = scatter_rows(unproject(d_qkv[:, :share_len]), d_x_send)
    input_grad = DEEP_ALPHA * d_z_one + d_x

    norm_terms = all_sum(
        jnp.stack([d_gain_one, d_bias_one, d_gain_two, d_bias_two]), ("dp", "obj", "tp")
    )
    local = width // lax.axis_size("tp")
    norm_terms = lax.dynamic_slice_in_dim(norm_terms, tp_index * local, local, 1)
    return (
        outputs[None],
        input_grad[None],
        jnp.stack([in_order(g, 0) for g in grad_qkv], axis=1),
        in_order(grad_out, 1),
        norm_terms[0],
        norm_terms[1],
        jnp.stack([in_order(g, 0) for g in grad_gate_up], axis=1),
        in_order(grad_down, 1),
        norm_terms[2],
        norm_terms[3],
    )


def solution(mesh):
    return jax.shard_map(
        body,
        mesh=mesh,
        in_specs=(
            P(("obj", "dp"), "tp", None),
            P(("obj", "dp"), "tp", None),
            P(("obj", "dp"), "tp"),
            P(("obj", "dp")),
            P(None, None, "tp"),
            P("tp", None),
            P(),
            P(),
            P(None, None, "tp"),
            P("tp", None),
            P(),
            P(),
        ),
        out_specs=(
            P(("obj", "dp"), "tp", None),
            P(("obj", "dp"), "tp", None),
            P(None, None, "tp"),
            P("tp", None),
            P("tp"),
            P("tp"),
            P(None, None, "tp"),
            P("tp", None),
            P("tp"),
            P("tp"),
        ),
        check_vma=False,
    )
```

```python
import functools

import jax
import jax.numpy as jnp
from jax import lax
from jax.experimental import pallas as pl
from jax.experimental.pallas import tpu as pltpu
from jax.sharding import PartitionSpec as P

HEAD_DIM = 128
DEEP_ALPHA = 48.0**0.5
NORM_EPS = 1e-05
MASKED_SCORE = -1e30
F32 = jnp.float32
BF16 = jnp.bfloat16
VMEM_BYTES = 60 * 1024 * 1024


def rotated(block, cos_ref, sin_ref, sign):
    half = block.shape[-1] // 2
    return block * cos_ref[...] + sign * (pltpu.roll(block, half, 1) * sin_ref[...])


def row_limits(info_ref, start, rows, seq_len):
    row_ids = lax.broadcasted_iota(jnp.int32, (1, rows), 1) + start + info_ref[0]
    row_ids = jnp.where(row_ids >= seq_len, row_ids - seq_len, row_ids)
    return jnp.maximum(row_ids, info_ref[1] - 1)


def key_ids(info_ref, seq_len):
    ids = lax.broadcasted_iota(jnp.int32, (seq_len, 1), 0) + info_ref[0]
    return jnp.where(ids >= seq_len, ids - seq_len, ids)


def attend_kernel(
    block_rows, info_ref, own_ref, other_ref, cos_ref, sin_ref, mixed_ref, qkv_ref
):
    share_len = own_ref.shape[1]
    seq_len = mixed_ref.shape[0]
    scale = HEAD_DIM**-0.5
    for part in range(3):
        block = jnp.concatenate([own_ref[part], other_ref[part]], axis=0)
        if part < 2:
            block = rotated(block, cos_ref, sin_ref, 1.0)
        qkv_ref[part] = block.astype(BF16)
    keys = qkv_ref[1]
    values = qkv_ref[2]
    ids = key_ids(info_ref, seq_len)
    for start in range(0, seq_len, block_rows):
        queries = qkv_ref[0, start : start + block_rows, :]
        scores = (
            lax.dot_general(keys, queries, (((1,), (1,)), ((), ())), preferred_element_type=F32)
            * scale
        )
        limits = row_limits(info_ref, start, block_rows, seq_len)
        scores = jnp.where(ids <= limits, scores, MASKED_SCORE)
        row_max = jnp.max(scores, axis=0, keepdims=True)
        weights = jnp.exp(scores - row_max)
        total = jnp.sum(weights, axis=0, keepdims=True)
        probs = (weights * (1.0 / total)).astype(BF16)
        mixed = lax.dot_general(
            probs, values, (((0,), (0,)), ((), ())), preferred_element_type=F32
        )
        mixed_ref[start : start + block_rows, :] = mixed.astype(BF16)


def attend_back_kernel(
    block_rows, info_ref, qkv_ref, grad_ref, cos_ref, sin_ref, out_ref, d_key_ref, d_value_ref
):
    seq_len = grad_ref.shape[0]
    scale = HEAD_DIM**-0.5
    keys = qkv_ref[1]
    values = qkv_ref[2]
    ids = key_ids(info_ref, seq_len)
    for start in range(0, seq_len, block_rows):
        rows = slice(start, start + block_rows)
        queries = qkv_ref[0, rows, :]
        grads = grad_ref[rows, :]
        scores = (
            lax.dot_general(keys, queries, (((1,), (1,)), ((), ())), preferred_element_type=F32)
            * scale
        )
        limits = row_limits(info_ref, start, block_rows, seq_len)
        scores = jnp.where(ids <= limits, scores, MASKED_SCORE)
        row_max = jnp.max(scores, axis=0, keepdims=True)
        weights = jnp.exp(scores - row_max)
        total = jnp.sum(weights, axis=0, keepdims=True)
        probs = weights * (1.0 / total)
        d_probs = lax.dot_general(
            values, grads, (((1,), (1,)), ((), ())), preferred_element_type=F32
        )
        delta = jnp.sum(probs * d_probs, axis=0, keepdims=True)
        d_scores = (probs * (d_probs - delta)).astype(BF16)
        d_value = jnp.dot(probs.astype(BF16), grads, preferred_element_type=F32)
        d_key = jnp.dot(d_scores, queries, preferred_element_type=F32)
        if start == 0:
            d_value_ref[...] = d_value
            d_key_ref[...] = d_key
        else:
            d_value_ref[...] += d_value
            d_key_ref[...] += d_key
        d_query = (
            lax.dot_general(d_scores, keys, (((0,), (0,)), ((), ())), preferred_element_type=F32)
            * scale
        )
        d_query = d_query * cos_ref[rows, :] - (
            pltpu.roll(d_query, HEAD_DIM // 2, 1) * sin_ref[rows, :]
        )
        out_ref[0, rows, :] = d_query.astype(BF16)
    d_key = d_key_ref[...] * scale
    out_ref[1] = rotated(d_key, cos_ref, sin_ref, -1.0).astype(BF16)
    out_ref[2] = d_value_ref[...].astype(BF16)


def attend(info, own, other, cos_vals, sin_vals):
    share_len, local_width = own.shape[1:]
    seq_len = share_len + other.shape[1]
    heads = local_width // HEAD_DIM
    table = pl.BlockSpec((seq_len, HEAD_DIM), lambda h, info: (0, 0))
    return pl.pallas_call(
        functools.partial(attend_kernel, min(256, seq_len)),
        grid_spec=pltpu.PrefetchScalarGridSpec(
            num_scalar_prefetch=1,
            grid=(heads,),
            in_specs=[
                pl.BlockSpec((3, share_len, HEAD_DIM), lambda h, info: (0, 0, h)),
                pl.BlockSpec((3, seq_len - share_len, HEAD_DIM), lambda h, info: (0, 0, h)),
                table,
                table,
            ],
            out_specs=[
                pl.BlockSpec((seq_len, HEAD_DIM), lambda h, info: (0, h)),
                pl.BlockSpec((3, seq_len, HEAD_DIM), lambda h, info: (0, 0, h)),
            ],
        ),
        out_shape=[
            jax.ShapeDtypeStruct((seq_len, local_width), BF16),
            jax.ShapeDtypeStruct((3, seq_len, local_width), BF16),
        ],
        compiler_params=pltpu.CompilerParams(vmem_limit_bytes=VMEM_BYTES),
        cost_estimate=pl.CostEstimate(
            flops=8 * seq_len * seq_len * local_width,
            bytes_accessed=seq_len * local_width * 20,
            transcendentals=seq_len * seq_len * heads,
        ),
        name="attend",
    )(info, own, other, cos_vals, sin_vals)


def attend_back(info, qkv, grads, cos_vals, sin_vals):
    seq_len, local_width = grads.shape
    heads = local_width // HEAD_DIM
    table = pl.BlockSpec((seq_len, HEAD_DIM), lambda h, info: (0, 0))
    return pl.pallas_call(
        functools.partial(attend_back_kernel, min(256, seq_len)),
        grid_spec=pltpu.PrefetchScalarGridSpec(
            num_scalar_prefetch=1,
            grid=(heads,),
            in_specs=[
                pl.BlockSpec((3, seq_len, HEAD_DIM), lambda h, info: (0, 0, h)),
                pl.BlockSpec((seq_len, HEAD_DIM), lambda h, info: (0, h)),
                table,
                table,
            ],
            out_specs=pl.BlockSpec((3, seq_len, HEAD_DIM), lambda h, info: (0, 0, h)),
            scratch_shapes=[
                pltpu.VMEM((seq_len, HEAD_DIM), F32),
                pltpu.VMEM((seq_len, HEAD_DIM), F32),
            ],
        ),
        out_shape=jax.ShapeDtypeStruct((3, seq_len, local_width), BF16),
        compiler_params=pltpu.CompilerParams(vmem_limit_bytes=VMEM_BYTES),
        cost_estimate=pl.CostEstimate(
            flops=20 * seq_len * seq_len * local_width,
            bytes_accessed=seq_len * local_width * 14,
            transcendentals=seq_len * seq_len * heads,
        ),
        name="attend_back",
    )(info, qkv, grads, cos_vals, sin_vals)


def gather_rows(own):
    size = lax.axis_size("tp")
    if size == 2:
        return lax.ppermute(own, "tp", [(0, 1), (1, 0)])
    share = own.shape[0]
    whole = lax.all_gather(own, "tp", axis=0, tiled=True)
    start = (lax.axis_index("tp") + 1) * share
    return lax.dynamic_slice_in_dim(
        jnp.concatenate([whole, whole], axis=0), start, (size - 1) * share, 0
    )


def scatter_rows(own_part, send_part):
    size = lax.axis_size("tp")
    if size == 2:
        return own_part + lax.ppermute(send_part, "tp", [(0, 1), (1, 0)]).astype(F32)
    share = own_part.shape[0]
    ring = jnp.concatenate([own_part.astype(BF16), send_part] * 2, axis=0)
    start = (size - lax.axis_index("tp")) * share
    whole = lax.dynamic_slice_in_dim(ring, start, size * share, 0)
    return lax.psum_scatter(whole.astype(F32), "tp", scatter_dimension=0, tiled=True)


def all_sum(value, axes):
    for axis in axes:
        size = lax.axis_size(axis)
        step = 1
        while step < size:
            value = value + lax.ppermute(value, axis, [(i, i ^ step) for i in range(size)])
            step *= 2
    return value


GROUP = ("obj", "dp")


def reduce_share(partial):
    return lax.psum_scatter(partial.astype(BF16), GROUP, scatter_dimension=0, tiled=True)


def gather_shares(share):
    return lax.all_gather(share, GROUP, axis=0, tiled=True)


def gather_after(share, earlier):
    share, earlier = lax.optimization_barrier((share, earlier))
    return gather_shares(share), earlier


def token_sum(left, right):
    return lax.dot_general(left, right, (((0,), (0,)), ((), ())), preferred_element_type=F32)


def norm_stats(rows):
    mean = jnp.mean(rows, axis=-1, keepdims=True)
    centred = rows - mean
    scale = lax.rsqrt(jnp.mean(centred * centred, axis=-1, keepdims=True) + NORM_EPS)
    return centred * scale, scale


def norm_back(grads, zhat, scale, gain):
    q = grads * gain
    d_rows = scale * (
        q - jnp.mean(q, axis=-1, keepdims=True) - zhat * jnp.mean(q * zhat, axis=-1, keepdims=True)
    )
    return d_rows, jnp.sum(grads * zhat, axis=0), jnp.sum(grads, axis=0)


def body(
    hidden_in,
    cotangent,
    loss_mask,
    prefix_len,
    w_qkv,
    w_out,
    gain_one,
    bias_one,
    w_gate_up,
    w_down,
    gain_two,
    bias_two,
):
    tp_index = lax.axis_index("tp")
    share_len, width = hidden_in.shape[1:]
    seq_len = share_len * lax.axis_size("tp")
    local_ff = w_down.shape[0]
    mask_vals = loss_mask[0].astype(F32)
    total_count = all_sum(jnp.full((8, 128), jnp.sum(mask_vals)), ("dp", "tp"))[0, 0]

    positions = (tp_index * share_len + jnp.arange(seq_len, dtype=jnp.int32)) % seq_len
    half = HEAD_DIM // 2
    frequency = 10000.0 ** (-jnp.arange(half).astype(F32) / half)
    angles = positions.astype(F32)[:, None] * frequency[None, :]
    cos_half, sin_half = jnp.cos(angles), jnp.sin(angles)
    cos_vals = jnp.concatenate([cos_half, cos_half], axis=1)
    sin_vals = jnp.concatenate([-sin_half, sin_half], axis=1)
    info = jnp.stack([tp_index * share_len, prefix_len[0]]).astype(jnp.int32)

    def project(rows):
        return jnp.einsum("td,dke->kte", rows, w_qkv, preferred_element_type=F32)

    x_own = hidden_in[0]
    x_other = gather_rows(x_own)
    mixed, qkv = attend(info, project(x_own), project(x_other), cos_vals, sin_vals)
    mixed_own, mixed_other = mixed[:share_len], mixed[share_len:]
    out_send = jnp.dot(mixed_other, w_out, preferred_element_type=F32).astype(BF16)
    out_own = jnp.dot(mixed_own, w_out, preferred_element_type=F32)
    z_one = DEEP_ALPHA * x_own.astype(F32) + scatter_rows(out_own, out_send)
    zhat_one, scale_one = norm_stats(z_one)
    h_one = zhat_one * gain_one + bias_one
    h_own = h_one.astype(BF16)
    h_other = gather_rows(h_own)

    def feed(rows):
        gate_up = jnp.einsum("td,dke->tke", rows, w_gate_up, preferred_element_type=F32)
        gate, up = gate_up[:, 0], gate_up[:, 1]
        phi = 0.5 * (1.0 + lax.erf(gate * (0.5**0.5)))
        density = jnp.exp(-0.5 * gate * gate) * (0.5 / jnp.pi) ** 0.5
        act = gate * phi
        return lax.optimization_barrier(
            ((act * up).astype(BF16), up * (phi + gate * density), act)
        )

    hidden_own, slope_own, act_own = feed(h_own)
    hidden_other, slope_other, act_other = feed(h_other)
    ffn_send = jnp.dot(hidden_other, w_down, preferred_element_type=F32).astype(BF16)
    ffn_own = jnp.dot(hidden_own, w_down, preferred_element_type=F32)
    z_two = DEEP_ALPHA * h_one + scatter_rows(ffn_own, ffn_send)
    zhat_two, scale_two = norm_stats(z_two)
    outputs = (zhat_two * gain_two + bias_two).astype(BF16)
    grad_y = cotangent[0].astype(F32) * (mask_vals * (seq_len / total_count))[:, None]
    d_z_two, d_gain_two, d_bias_two = norm_back(grad_y, zhat_two, scale_two, gain_two)

    d_ffn_own = d_z_two.astype(BF16)
    d_ffn_other = gather_rows(d_ffn_own)
    hidden = jnp.concatenate([hidden_own, hidden_other], axis=0)
    d_ffn = jnp.concatenate([d_ffn_own, d_ffn_other], axis=0)

    def feed_back(d_rows, slope, act):
        d_hidden = lax.dot_general(
            d_rows, w_down, (((1,), (1,)), ((), ())), preferred_element_type=F32
        )
        return jnp.stack([d_hidden * slope, d_hidden * act], axis=0).astype(BF16)

    partial_down, d_ffn_own, d_ffn_other = lax.optimization_barrier(
        (token_sum(hidden, d_ffn).astype(BF16), d_ffn_own, d_ffn_other)
    )
    share_down = reduce_share(partial_down)
    d_gu_own = feed_back(d_ffn_own, slope_own, act_own)
    d_gu_other = feed_back(d_ffn_other, slope_other, act_other)
    d_gu = jnp.concatenate([d_gu_own, d_gu_other], axis=1)
    h_rows = jnp.concatenate([h_own, h_other], axis=0)
    partial_gate_up = [token_sum(h_rows, d_gu[k]).astype(BF16) for k in range(2)]

    def feed_rows(d_gate_up):
        return jnp.einsum("kte,dke->td", d_gate_up, w_gate_up, preferred_element_type=F32)

    d_h_send = feed_rows(d_gu_other).astype(BF16)
    d_h = scatter_rows(feed_rows(d_gu_own), d_h_send)
    d_h, partial_gate_up[0] = lax.optimization_barrier((d_h, partial_gate_up[0]))
    d_z_one, d_gain_one, d_bias_one = norm_back(
        DEEP_ALPHA * d_z_two + d_h, zhat_one, scale_one, gain_one
    )
    d_attn_own = d_z_one.astype(BF16)
    d_attn_other, partial_gate_up[1] = lax.optimization_barrier(
        (gather_rows(d_attn_own), partial_gate_up[1])
    )
    share_gate_up = [reduce_share(partial) for partial in partial_gate_up]
    d_attn = jnp.concatenate([d_attn_own, d_attn_other], axis=0)
    partial_out, d_attn_own, d_attn_other = lax.optimization_barrier(
        (token_sum(mixed, d_attn).astype(BF16), d_attn_own, d_attn_other)
    )
    share_out = reduce_share(partial_out)

    def unmix(d_rows):
        return lax.dot_general(
            d_rows, w_out, (((1,), (1,)), ((), ())), preferred_element_type=F32
        ).astype(BF16)

    d_mixed = jnp.concatenate([unmix(d_attn_own), unmix(d_attn_other)], axis=0)
    d_mixed, share_down = lax.optimization_barrier((d_mixed, share_down))
    d_qkv = attend_back(info, qkv, d_mixed, cos_vals, sin_vals)
    d_qkv, share_gate_up[0] = lax.optimization_barrier((d_qkv, share_gate_up[0]))
    x_rows = jnp.concatenate([x_own, x_other], axis=0)
    partial_qkv = [token_sum(x_rows, d_qkv[k]).astype(BF16) for k in range(3)]

    def unproject(d_rows):
        return jnp.einsum("kte,dke->td", d_rows, w_qkv, preferred_element_type=F32)

    d_x_send = unproject(d_qkv[:, share_len:]).astype(BF16)
    d_x_send, share_gate_up[1], share_out, partial_qkv = lax.optimization_barrier(
        (d_x_send, share_gate_up[1], share_out, partial_qkv)
    )
    share_qkv = [reduce_share(partial) for partial in partial_qkv]
    d_x = scatter_rows(unproject(d_qkv[:, :share_len]), d_x_send)
    input_grad = DEEP_ALPHA * d_z_one + d_x

    norm_terms = all_sum(
        jnp.stack([d_gain_one, d_bias_one, d_gain_two, d_bias_two]), ("dp", "obj", "tp")
    )
    local = width // lax.axis_size("tp")
    norm_terms = lax.dynamic_slice_in_dim(norm_terms, tp_index * local, local, 1)

    share_gate_up = jnp.stack(share_gate_up, axis=1)
    share_qkv = jnp.concatenate(share_qkv, axis=1)
    share_rows = jnp.concatenate([share_down, share_out], axis=0)
    input_grad, share_gate_up, share_qkv, share_rows = lax.optimization_barrier(
        (input_grad, share_gate_up, share_qkv, share_rows)
    )
    grad_gate_up = gather_shares(share_gate_up)
    grad_qkv, grad_gate_up = gather_after(share_qkv, grad_gate_up)
    grad_rows, grad_qkv = gather_after(share_rows, grad_qkv)
    grad_gate_up = grad_gate_up.astype(F32)
    grad_qkv = jnp.stack(jnp.split(grad_qkv, 3, axis=1), axis=1).astype(F32)
    group_size = lax.axis_size(GROUP)
    grad_rows = grad_rows.reshape(group_size, -1, width).astype(F32)
    down_rows = local_ff // group_size
    grad_down = grad_rows[:, :down_rows].reshape(-1, width)
    grad_out = grad_rows[:, down_rows:].reshape(-1, width)
    return (
        outputs[None],
        input_grad[None],
        grad_qkv,
        grad_out,
        norm_terms[0],
        norm_terms[1],
        grad_gate_up,
        grad_down,
        norm_terms[2],
        norm_terms[3],
    )


def solution(mesh):
    return jax.shard_map(
        body,
        mesh=mesh,
        in_specs=(
            P(("obj", "dp"), "tp", None),
            P(("obj", "dp"), "tp", None),
            P(("obj", "dp"), "tp"),
            P(("obj", "dp")),
            P(None, None, "tp"),
            P("tp", None),
            P(),
            P(),
            P(None, None, "tp"),
            P("tp", None),
            P(),
            P(),
        ),
        out_specs=(
            P(("obj", "dp"), "tp", None),
            P(("obj", "dp"), "tp", None),
            P(None, None, "tp"),
            P("tp", None),
            P("tp"),
            P("tp"),
            P(None, None, "tp"),
            P("tp", None),
            P("tp"),
            P("tp"),
        ),
        check_vma=False,
    )
```

```python
import functools

import jax
import jax.numpy as jnp
from jax import lax
from jax.experimental import pallas as pl
from jax.experimental.pallas import tpu as pltpu
from jax.sharding import PartitionSpec as P

HEAD_DIM = 128
DEEP_ALPHA = 48.0**0.5
NORM_EPS = 1e-05
MASKED_SCORE = -1e30
F32 = jnp.float32
BF16 = jnp.bfloat16
VMEM_BYTES = 60 * 1024 * 1024


def rotated(block, cos_ref, sin_ref, sign):
    half = block.shape[-1] // 2
    return block * cos_ref[...] + sign * (pltpu.roll(block, half, 1) * sin_ref[...])


def row_limits(info_ref, start, rows, seq_len):
    row_ids = lax.broadcasted_iota(jnp.int32, (1, rows), 1) + start + info_ref[0]
    row_ids = jnp.where(row_ids >= seq_len, row_ids - seq_len, row_ids)
    return jnp.maximum(row_ids, info_ref[1] - 1)


def key_ids(info_ref, seq_len):
    ids = lax.broadcasted_iota(jnp.int32, (seq_len, 1), 0) + info_ref[0]
    return jnp.where(ids >= seq_len, ids - seq_len, ids)


def attend_kernel(
    block_rows, info_ref, own_ref, other_ref, cos_ref, sin_ref, mixed_ref, qkv_ref
):
    share_len = own_ref.shape[1]
    seq_len = mixed_ref.shape[0]
    scale = HEAD_DIM**-0.5
    for part in range(3):
        block = jnp.concatenate([own_ref[part], other_ref[part]], axis=0)
        if part < 2:
            block = rotated(block, cos_ref, sin_ref, 1.0)
        qkv_ref[part] = block.astype(BF16)
    keys = qkv_ref[1]
    values = qkv_ref[2]
    ids = key_ids(info_ref, seq_len)
    for start in range(0, seq_len, block_rows):
        queries = qkv_ref[0, start : start + block_rows, :]
        scores = (
            lax.dot_general(keys, queries, (((1,), (1,)), ((), ())), preferred_element_type=F32)
            * scale
        )
        limits = row_limits(info_ref, start, block_rows, seq_len)
        scores = jnp.where(ids <= limits, scores, MASKED_SCORE)
        row_max = jnp.max(scores, axis=0, keepdims=True)
        weights = jnp.exp(scores - row_max)
        total = jnp.sum(weights, axis=0, keepdims=True)
        probs = (weights * (1.0 / total)).astype(BF16)
        mixed = lax.dot_general(
            probs, values, (((0,), (0,)), ((), ())), preferred_element_type=F32
        )
        mixed_ref[start : start + block_rows, :] = mixed.astype(BF16)


def attend_back_kernel(
    block_rows, info_ref, qkv_ref, grad_ref, cos_ref, sin_ref, out_ref, d_key_ref, d_value_ref
):
    seq_len = grad_ref.shape[0]
    scale = HEAD_DIM**-0.5
    keys = qkv_ref[1]
    values = qkv_ref[2]
    ids = key_ids(info_ref, seq_len)
    for start in range(0, seq_len, block_rows):
        rows = slice(start, start + block_rows)
        queries = qkv_ref[0, rows, :]
        grads = grad_ref[rows, :]
        scores = (
            lax.dot_general(keys, queries, (((1,), (1,)), ((), ())), preferred_element_type=F32)
            * scale
        )
        limits = row_limits(info_ref, start, block_rows, seq_len)
        scores = jnp.where(ids <= limits, scores, MASKED_SCORE)
        row_max = jnp.max(scores, axis=0, keepdims=True)
        weights = jnp.exp(scores - row_max)
        total = jnp.sum(weights, axis=0, keepdims=True)
        probs = weights * (1.0 / total)
        d_probs = lax.dot_general(
            values, grads, (((1,), (1,)), ((), ())), preferred_element_type=F32
        )
        delta = jnp.sum(probs * d_probs, axis=0, keepdims=True)
        d_scores = (probs * (d_probs - delta)).astype(BF16)
        d_value = jnp.dot(probs.astype(BF16), grads, preferred_element_type=F32)
        d_key = jnp.dot(d_scores, queries, preferred_element_type=F32)
        if start == 0:
            d_value_ref[...] = d_value
            d_key_ref[...] = d_key
        else:
            d_value_ref[...] += d_value
            d_key_ref[...] += d_key
        d_query = (
            lax.dot_general(d_scores, keys, (((0,), (0,)), ((), ())), preferred_element_type=F32)
            * scale
        )
        d_query = d_query * cos_ref[rows, :] - (
            pltpu.roll(d_query, HEAD_DIM // 2, 1) * sin_ref[rows, :]
        )
        out_ref[0, rows, :] = d_query.astype(BF16)
    d_key = d_key_ref[...] * scale
    out_ref[1] = rotated(d_key, cos_ref, sin_ref, -1.0).astype(BF16)
    out_ref[2] = d_value_ref[...].astype(BF16)


def attend(info, own, other, cos_vals, sin_vals):
    share_len, local_width = own.shape[1:]
    seq_len = share_len + other.shape[1]
    heads = local_width // HEAD_DIM
    table = pl.BlockSpec((seq_len, HEAD_DIM), lambda h, info: (0, 0))
    return pl.pallas_call(
        functools.partial(attend_kernel, min(256, seq_len)),
        grid_spec=pltpu.PrefetchScalarGridSpec(
            num_scalar_prefetch=1,
            grid=(heads,),
            in_specs=[
                pl.BlockSpec((3, share_len, HEAD_DIM), lambda h, info: (0, 0, h)),
                pl.BlockSpec((3, seq_len - share_len, HEAD_DIM), lambda h, info: (0, 0, h)),
                table,
                table,
            ],
            out_specs=[
                pl.BlockSpec((seq_len, HEAD_DIM), lambda h, info: (0, h)),
                pl.BlockSpec((3, seq_len, HEAD_DIM), lambda h, info: (0, 0, h)),
            ],
        ),
        out_shape=[
            jax.ShapeDtypeStruct((seq_len, local_width), BF16),
            jax.ShapeDtypeStruct((3, seq_len, local_width), BF16),
        ],
        compiler_params=pltpu.CompilerParams(vmem_limit_bytes=VMEM_BYTES),
        cost_estimate=pl.CostEstimate(
            flops=8 * seq_len * seq_len * local_width,
            bytes_accessed=seq_len * local_width * 20,
            transcendentals=seq_len * seq_len * heads,
        ),
        name="attend",
    )(info, own, other, cos_vals, sin_vals)


def attend_back(info, qkv, grads, cos_vals, sin_vals):
    seq_len, local_width = grads.shape
    heads = local_width // HEAD_DIM
    table = pl.BlockSpec((seq_len, HEAD_DIM), lambda h, info: (0, 0))
    return pl.pallas_call(
        functools.partial(attend_back_kernel, min(256, seq_len)),
        grid_spec=pltpu.PrefetchScalarGridSpec(
            num_scalar_prefetch=1,
            grid=(heads,),
            in_specs=[
                pl.BlockSpec((3, seq_len, HEAD_DIM), lambda h, info: (0, 0, h)),
                pl.BlockSpec((seq_len, HEAD_DIM), lambda h, info: (0, h)),
                table,
                table,
            ],
            out_specs=pl.BlockSpec((3, seq_len, HEAD_DIM), lambda h, info: (0, 0, h)),
            scratch_shapes=[
                pltpu.VMEM((seq_len, HEAD_DIM), F32),
                pltpu.VMEM((seq_len, HEAD_DIM), F32),
            ],
        ),
        out_shape=jax.ShapeDtypeStruct((3, seq_len, local_width), BF16),
        compiler_params=pltpu.CompilerParams(vmem_limit_bytes=VMEM_BYTES),
        cost_estimate=pl.CostEstimate(
            flops=20 * seq_len * seq_len * local_width,
            bytes_accessed=seq_len * local_width * 14,
            transcendentals=seq_len * seq_len * heads,
        ),
        name="attend_back",
    )(info, qkv, grads, cos_vals, sin_vals)


def gather_rows(own):
    size = lax.axis_size("tp")
    if size == 2:
        return lax.ppermute(own, "tp", [(0, 1), (1, 0)])
    share = own.shape[0]
    whole = lax.all_gather(own, "tp", axis=0, tiled=True)
    start = (lax.axis_index("tp") + 1) * share
    return lax.dynamic_slice_in_dim(
        jnp.concatenate([whole, whole], axis=0), start, (size - 1) * share, 0
    )


def scatter_rows(own_part, send_part):
    size = lax.axis_size("tp")
    if size == 2:
        return own_part + lax.ppermute(send_part, "tp", [(0, 1), (1, 0)]).astype(F32)
    share = own_part.shape[0]
    ring = jnp.concatenate([own_part.astype(BF16), send_part] * 2, axis=0)
    start = (size - lax.axis_index("tp")) * share
    whole = lax.dynamic_slice_in_dim(ring, start, size * share, 0)
    return lax.psum_scatter(whole.astype(F32), "tp", scatter_dimension=0, tiled=True)


def all_sum(value, axes):
    for axis in axes:
        size = lax.axis_size(axis)
        step = 1
        while step < size:
            value = value + lax.ppermute(value, axis, [(i, i ^ step) for i in range(size)])
            step *= 2
    return value


CORE_SWAP = [(0, 1), (1, 0), (2, 3), (3, 2)]
X_SWAP = [(0, 2), (2, 0), (1, 3), (3, 1)]
Z_NEAR = [(0, 1), (1, 0), (2, 3), (3, 2)]
Z_FAR = [(0, 2), (2, 0), (1, 3), (3, 1)]
GROUP = ("dp", "obj")
tie = lax.optimization_barrier


def columns(array, index, count=4):
    width = array.shape[-1] // count
    return lax.dynamic_slice_in_dim(array, index * width, width, array.ndim - 1)


def give_quarters(make):
    dp_index = lax.axis_index("dp")
    return make(3 - dp_index).astype(BF16), make(dp_index ^ 1).astype(BF16)


def core_stage(make, gives):
    dp_index = lax.axis_index("dp")
    got_far = lax.ppermute(gives[0], "dp", CORE_SWAP)
    got_near = lax.ppermute(gives[1], "dp", CORE_SWAP)
    far = (make(dp_index ^ 2) + got_far.astype(F32)).astype(BF16)
    return far, make(dp_index) + got_near.astype(F32)


def x_stage(far, near):
    return near + lax.ppermute(far, "dp", X_SWAP).astype(F32)


def z_near_stage(near, axis):
    obj_index = lax.axis_index("obj")
    width = near.shape[axis] // lax.axis_size("obj")

    def pieces(first):
        return jnp.stack(
            [
                lax.dynamic_slice_in_dim(near, index * width, width, axis)
                for index in (first, first ^ 2)
            ]
        )

    got = lax.ppermute(pieces(obj_index ^ 1).astype(BF16), "obj", Z_NEAR)
    return pieces(obj_index) + got.astype(F32)


def z_far_stage(pair):
    got = lax.ppermute(pair[1].astype(BF16), "obj", Z_FAR)
    return (pair[0] + got.astype(F32)).astype(BF16)


def gather_rows_of(share):
    return lax.all_gather(share, GROUP, axis=0, tiled=True)


def gather_columns_of(share):
    return lax.all_gather(share, GROUP, axis=0, tiled=False)


def widen(stacked):
    return jnp.concatenate([stacked[i] for i in range(stacked.shape[0])], axis=1).astype(F32)


def token_sum(left, right):
    return lax.dot_general(left, right, (((0,), (0,)), ((), ())), preferred_element_type=F32)


def norm_stats(rows):
    mean = jnp.mean(rows, axis=-1, keepdims=True)
    centred = rows - mean
    scale = lax.rsqrt(jnp.mean(centred * centred, axis=-1, keepdims=True) + NORM_EPS)
    return centred * scale, scale


def norm_back(grads, zhat, scale, gain):
    q = grads * gain
    d_rows = scale * (
        q - jnp.mean(q, axis=-1, keepdims=True) - zhat * jnp.mean(q * zhat, axis=-1, keepdims=True)
    )
    return d_rows, jnp.sum(grads * zhat, axis=0), jnp.sum(grads, axis=0)


def body(
    hidden_in,
    cotangent,
    loss_mask,
    prefix_len,
    w_qkv,
    w_out,
    gain_one,
    bias_one,
    w_gate_up,
    w_down,
    gain_two,
    bias_two,
):
    tp_index = lax.axis_index("tp")
    share_len, width = hidden_in.shape[1:]
    seq_len = share_len * lax.axis_size("tp")
    local_ff = w_down.shape[0]
    mask_vals = loss_mask[0].astype(F32)
    total_count = all_sum(jnp.full((8, 128), jnp.sum(mask_vals)), ("dp", "tp"))[0, 0]

    positions = (tp_index * share_len + jnp.arange(seq_len, dtype=jnp.int32)) % seq_len
    half = HEAD_DIM // 2
    frequency = 10000.0 ** (-jnp.arange(half).astype(F32) / half)
    angles = positions.astype(F32)[:, None] * frequency[None, :]
    cos_half, sin_half = jnp.cos(angles), jnp.sin(angles)
    cos_vals = jnp.concatenate([cos_half, cos_half], axis=1)
    sin_vals = jnp.concatenate([-sin_half, sin_half], axis=1)
    info = jnp.stack([tp_index * share_len, prefix_len[0]]).astype(jnp.int32)

    def project(rows):
        return jnp.einsum("td,dke->kte", rows, w_qkv, preferred_element_type=F32)

    x_own = hidden_in[0]
    x_other = gather_rows(x_own)
    mixed, qkv = attend(info, project(x_own), project(x_other), cos_vals, sin_vals)
    mixed_own, mixed_other = mixed[:share_len], mixed[share_len:]
    out_send = jnp.dot(mixed_other, w_out, preferred_element_type=F32).astype(BF16)
    out_own = jnp.dot(mixed_own, w_out, preferred_element_type=F32)
    z_one = DEEP_ALPHA * x_own.astype(F32) + scatter_rows(out_own, out_send)
    zhat_one, scale_one = norm_stats(z_one)
    h_one = zhat_one * gain_one + bias_one
    h_own = h_one.astype(BF16)
    h_other = gather_rows(h_own)

    def feed(rows):
        gate_up = jnp.einsum("td,dke->tke", rows, w_gate_up, preferred_element_type=F32)
        gate, up = gate_up[:, 0], gate_up[:, 1]
        phi = 0.5 * (1.0 + lax.erf(gate * (0.5**0.5)))
        density = jnp.exp(-0.5 * gate * gate) * (0.5 / jnp.pi) ** 0.5
        act = gate * phi
        return lax.optimization_barrier(
            ((act * up).astype(BF16), up * (phi + gate * density), act)
        )

    hidden_own, slope_own, act_own = feed(h_own)
    hidden_other, slope_other, act_other = feed(h_other)
    ffn_send = jnp.dot(hidden_other, w_down, preferred_element_type=F32).astype(BF16)
    ffn_own = jnp.dot(hidden_own, w_down, preferred_element_type=F32)
    z_two = DEEP_ALPHA * h_one + scatter_rows(ffn_own, ffn_send)
    zhat_two, scale_two = norm_stats(z_two)
    outputs = (zhat_two * gain_two + bias_two).astype(BF16)
    grad_y = cotangent[0].astype(F32) * (mask_vals * (seq_len / total_count))[:, None]
    d_z_two, d_gain_two, d_bias_two = norm_back(grad_y, zhat_two, scale_two, gain_two)

    d_ffn_own = d_z_two.astype(BF16)
    d_ffn_other = gather_rows(d_ffn_own)
    hidden = jnp.concatenate([hidden_own, hidden_other], axis=0)
    d_ffn = jnp.concatenate([d_ffn_own, d_ffn_other], axis=0)

    def feed_back(d_rows, slope, act):
        d_hidden = lax.dot_general(
            d_rows, w_down, (((1,), (1,)), ((), ())), preferred_element_type=F32
        )
        return jnp.stack([d_hidden * slope, d_hidden * act], axis=0).astype(BF16)

    def make_down(q):
        return token_sum(hidden, columns(d_ffn, q))

    gives_down, d_ffn_own, d_ffn_other = tie((give_quarters(make_down), d_ffn_own, d_ffn_other))
    d_gu_other = feed_back(d_ffn_other, slope_other, act_other)
    (far_down, near_down), d_gu_other = tie((core_stage(make_down, gives_down), d_gu_other))
    near_down = x_stage(far_down, near_down)

    def feed_rows(d_gate_up):
        return jnp.einsum("kte,dke->td", d_gate_up, w_gate_up, preferred_element_type=F32)

    d_h_send = feed_rows(d_gu_other).astype(BF16)
    d_gu_own = feed_back(d_ffn_own, slope_own, act_own)
    d_gu = jnp.concatenate([d_gu_own, d_gu_other], axis=1)
    h_rows = jnp.concatenate([h_own, h_other], axis=0)

    def make_gate(q):
        return token_sum(columns(h_rows, q), d_gu[0])

    def make_up(q):
        return token_sum(columns(h_rows, q), d_gu[1])

    d_h = scatter_rows(feed_rows(d_gu_own), d_h_send)
    d_h, (far_gate, near_gate) = tie((d_h, core_stage(make_gate, give_quarters(make_gate))))
    near_gate = x_stage(far_gate, near_gate)
    d_z_one, d_gain_one, d_bias_one = norm_back(
        DEEP_ALPHA * d_z_two + d_h, zhat_one, scale_one, gain_one
    )
    d_attn_own = d_z_one.astype(BF16)
    d_attn_other = gather_rows(d_attn_own)
    d_attn_other, (far_up, near_up), near_down = tie(
        (d_attn_other, core_stage(make_up, give_quarters(make_up)), near_down)
    )
    near_up = x_stage(far_up, near_up)
    pair_down = z_near_stage(near_down, 1)
    d_attn = jnp.concatenate([d_attn_own, d_attn_other], axis=0)

    def make_out(q):
        return token_sum(mixed, columns(d_attn, q))

    gives_out, d_attn_own, d_attn_other = tie((give_quarters(make_out), d_attn_own, d_attn_other))

    def unmix(d_rows):
        return lax.dot_general(
            d_rows, w_out, (((1,), (1,)), ((), ())), preferred_element_type=F32
        ).astype(BF16)

    d_mixed = jnp.concatenate([unmix(d_attn_own), unmix(d_attn_other)], axis=0)
    d_mixed, (far_out, near_out), near_gate, pair_down = tie(
        (d_mixed, core_stage(make_out, gives_out), near_gate, pair_down)
    )
    near_out = x_stage(far_out, near_out)
    pair_gate = z_near_stage(near_gate, 0)
    share_down = z_far_stage(pair_down)
    d_qkv = attend_back(info, qkv, d_mixed, cos_vals, sin_vals)
    d_qkv, near_up, pair_gate, share_down = tie((d_qkv, near_up, pair_gate, share_down))
    pair_up = z_near_stage(near_up, 0)
    share_gate = z_far_stage(pair_gate)
    x_rows = jnp.concatenate([x_own, x_other], axis=0)

    def make_qkv(k):
        return lambda q: token_sum(columns(x_rows, q), d_qkv[k])

    gives_qkv = [give_quarters(make_qkv(k)) for k in range(3)]

    def unproject(d_rows):
        return jnp.einsum("kte,dke->td", d_rows, w_qkv, preferred_element_type=F32)

    parts_qkv = [core_stage(make_qkv(k), gives_qkv[k]) for k in range(3)]
    parts_qkv, near_out = tie((parts_qkv, near_out))
    pair_out = z_near_stage(near_out, 1)
    near_qkv = [x_stage(far, near) for far, near in parts_qkv]
    d_x_send = unproject(d_qkv[:, share_len:]).astype(BF16)
    d_x_send, pair_up, share_gate = tie((d_x_send, pair_up, share_gate))
    near_qkv, pair_up, pair_out = tie((near_qkv, pair_up, pair_out))
    share_up = z_far_stage(pair_up)
    share_out = z_far_stage(pair_out)
    d_x = scatter_rows(unproject(d_qkv[:, :share_len]), d_x_send)
    input_grad = DEEP_ALPHA * d_z_one + d_x

    norm_terms = all_sum(
        jnp.stack([d_gain_one, d_bias_one, d_gain_two, d_bias_two]), ("dp", "obj", "tp")
    )
    local = width // lax.axis_size("tp")
    norm_terms = lax.dynamic_slice_in_dim(norm_terms, tp_index * local, local, 1)

    share_lanes = jnp.concatenate([share_down, share_out], axis=0)
    share_gate_up = jnp.stack([share_gate, share_up], axis=1)
    grad_lanes = gather_columns_of(share_lanes)
    grad_gate_up = gather_rows_of(share_gate_up)
    share_qkv = [z_far_stage(z_near_stage(near, 0)) for near in near_qkv]
    share_qkv, grad_lanes = tie((share_qkv, grad_lanes))
    grad_qkv = gather_rows_of(jnp.stack(share_qkv, axis=1)).astype(F32)
    grad_gate_up = grad_gate_up.astype(F32)
    grad_down = widen(grad_lanes[:, :local_ff])
    grad_out = widen(grad_lanes[:, local_ff:])
    return (
        outputs[None],
        input_grad[None],
        grad_qkv,
        grad_out,
        norm_terms[0],
        norm_terms[1],
        grad_gate_up,
        grad_down,
        norm_terms[2],
        norm_terms[3],
    )


def solution(mesh):
    return jax.shard_map(
        body,
        mesh=mesh,
        in_specs=(
            P(("obj", "dp"), "tp", None),
            P(("obj", "dp"), "tp", None),
            P(("obj", "dp"), "tp"),
            P(("obj", "dp")),
            P(None, None, "tp"),
            P("tp", None),
            P(),
            P(),
            P(None, None, "tp"),
            P("tp", None),
            P(),
            P(),
        ),
        out_specs=(
            P(("obj", "dp"), "tp", None),
            P(("obj", "dp"), "tp", None),
            P(None, None, "tp"),
            P("tp", None),
            P("tp"),
            P("tp"),
            P(None, None, "tp"),
            P("tp", None),
            P("tp"),
            P("tp"),
        ),
        check_vma=False,
    )
```

```python
import functools

import jax
import jax.numpy as jnp
from jax import lax
from jax.experimental import pallas as pl
from jax.experimental.pallas import tpu as pltpu
from jax.sharding import PartitionSpec as P

HEAD_DIM = 128
DEEP_ALPHA = 48.0**0.5
NORM_EPS = 1e-05
MASKED_SCORE = -1e30
F32 = jnp.float32
BF16 = jnp.bfloat16
VMEM_BYTES = 60 * 1024 * 1024


def rotated(block, cos_ref, sin_ref, sign):
    half = block.shape[-1] // 2
    return block * cos_ref[...] + sign * (pltpu.roll(block, half, 1) * sin_ref[...])


def row_limits(info_ref, start, rows, seq_len):
    row_ids = lax.broadcasted_iota(jnp.int32, (1, rows), 1) + start + info_ref[0]
    row_ids = jnp.where(row_ids >= seq_len, row_ids - seq_len, row_ids)
    return jnp.maximum(row_ids, info_ref[1] - 1)


def key_ids(info_ref, seq_len):
    ids = lax.broadcasted_iota(jnp.int32, (seq_len, 1), 0) + info_ref[0]
    return jnp.where(ids >= seq_len, ids - seq_len, ids)


def attend_kernel(
    block_rows, info_ref, own_ref, other_ref, cos_ref, sin_ref, mixed_ref, qkv_ref
):
    share_len = own_ref.shape[1]
    seq_len = mixed_ref.shape[0]
    scale = HEAD_DIM**-0.5
    for part in range(3):
        block = jnp.concatenate([own_ref[part], other_ref[part]], axis=0)
        if part < 2:
            block = rotated(block, cos_ref, sin_ref, 1.0)
        qkv_ref[part] = block.astype(BF16)
    keys = qkv_ref[1]
    values = qkv_ref[2]
    ids = key_ids(info_ref, seq_len)
    for start in range(0, seq_len, block_rows):
        queries = qkv_ref[0, start : start + block_rows, :]
        scores = (
            lax.dot_general(keys, queries, (((1,), (1,)), ((), ())), preferred_element_type=F32)
            * scale
        )
        limits = row_limits(info_ref, start, block_rows, seq_len)
        scores = jnp.where(ids <= limits, scores, MASKED_SCORE)
        row_max = jnp.max(scores, axis=0, keepdims=True)
        weights = jnp.exp(scores - row_max)
        total = jnp.sum(weights, axis=0, keepdims=True)
        probs = (weights * (1.0 / total)).astype(BF16)
        mixed = lax.dot_general(
            probs, values, (((0,), (0,)), ((), ())), preferred_element_type=F32
        )
        mixed_ref[start : start + block_rows, :] = mixed.astype(BF16)


def attend_back_kernel(
    block_rows, info_ref, qkv_ref, grad_ref, cos_ref, sin_ref, out_ref, d_key_ref, d_value_ref
):
    seq_len = grad_ref.shape[0]
    scale = HEAD_DIM**-0.5
    keys = qkv_ref[1]
    values = qkv_ref[2]
    ids = key_ids(info_ref, seq_len)
    for start in range(0, seq_len, block_rows):
        rows = slice(start, start + block_rows)
        queries = qkv_ref[0, rows, :]
        grads = grad_ref[rows, :]
        scores = (
            lax.dot_general(keys, queries, (((1,), (1,)), ((), ())), preferred_element_type=F32)
            * scale
        )
        limits = row_limits(info_ref, start, block_rows, seq_len)
        scores = jnp.where(ids <= limits, scores, MASKED_SCORE)
        row_max = jnp.max(scores, axis=0, keepdims=True)
        weights = jnp.exp(scores - row_max)
        total = jnp.sum(weights, axis=0, keepdims=True)
        probs = weights * (1.0 / total)
        d_probs = lax.dot_general(
            values, grads, (((1,), (1,)), ((), ())), preferred_element_type=F32
        )
        delta = jnp.sum(probs * d_probs, axis=0, keepdims=True)
        d_scores = (probs * (d_probs - delta)).astype(BF16)
        d_value = jnp.dot(probs.astype(BF16), grads, preferred_element_type=F32)
        d_key = jnp.dot(d_scores, queries, preferred_element_type=F32)
        if start == 0:
            d_value_ref[...] = d_value
            d_key_ref[...] = d_key
        else:
            d_value_ref[...] += d_value
            d_key_ref[...] += d_key
        d_query = (
            lax.dot_general(d_scores, keys, (((0,), (0,)), ((), ())), preferred_element_type=F32)
            * scale
        )
        d_query = d_query * cos_ref[rows, :] - (
            pltpu.roll(d_query, HEAD_DIM // 2, 1) * sin_ref[rows, :]
        )
        out_ref[0, rows, :] = d_query.astype(BF16)
    d_key = d_key_ref[...] * scale
    out_ref[1] = rotated(d_key, cos_ref, sin_ref, -1.0).astype(BF16)
    out_ref[2] = d_value_ref[...].astype(BF16)


def attend(info, own, other, cos_vals, sin_vals):
    share_len, local_width = own.shape[1:]
    seq_len = share_len + other.shape[1]
    heads = local_width // HEAD_DIM
    table = pl.BlockSpec((seq_len, HEAD_DIM), lambda h, info: (0, 0))
    return pl.pallas_call(
        functools.partial(attend_kernel, min(256, seq_len)),
        grid_spec=pltpu.PrefetchScalarGridSpec(
            num_scalar_prefetch=1,
            grid=(heads,),
            in_specs=[
                pl.BlockSpec((3, share_len, HEAD_DIM), lambda h, info: (0, 0, h)),
                pl.BlockSpec((3, seq_len - share_len, HEAD_DIM), lambda h, info: (0, 0, h)),
                table,
                table,
            ],
            out_specs=[
                pl.BlockSpec((seq_len, HEAD_DIM), lambda h, info: (0, h)),
                pl.BlockSpec((3, seq_len, HEAD_DIM), lambda h, info: (0, 0, h)),
            ],
        ),
        out_shape=[
            jax.ShapeDtypeStruct((seq_len, local_width), BF16),
            jax.ShapeDtypeStruct((3, seq_len, local_width), BF16),
        ],
        compiler_params=pltpu.CompilerParams(vmem_limit_bytes=VMEM_BYTES),
        cost_estimate=pl.CostEstimate(
            flops=8 * seq_len * seq_len * local_width,
            bytes_accessed=seq_len * local_width * 20,
            transcendentals=seq_len * seq_len * heads,
        ),
        name="attend",
    )(info, own, other, cos_vals, sin_vals)


def attend_back(info, qkv, grads, cos_vals, sin_vals):
    seq_len, local_width = grads.shape
    heads = local_width // HEAD_DIM
    table = pl.BlockSpec((seq_len, HEAD_DIM), lambda h, info: (0, 0))
    return pl.pallas_call(
        functools.partial(attend_back_kernel, min(256, seq_len)),
        grid_spec=pltpu.PrefetchScalarGridSpec(
            num_scalar_prefetch=1,
            grid=(heads,),
            in_specs=[
                pl.BlockSpec((3, seq_len, HEAD_DIM), lambda h, info: (0, 0, h)),
                pl.BlockSpec((seq_len, HEAD_DIM), lambda h, info: (0, h)),
                table,
                table,
            ],
            out_specs=pl.BlockSpec((3, seq_len, HEAD_DIM), lambda h, info: (0, 0, h)),
            scratch_shapes=[
                pltpu.VMEM((seq_len, HEAD_DIM), F32),
                pltpu.VMEM((seq_len, HEAD_DIM), F32),
            ],
        ),
        out_shape=jax.ShapeDtypeStruct((3, seq_len, local_width), BF16),
        compiler_params=pltpu.CompilerParams(vmem_limit_bytes=VMEM_BYTES),
        cost_estimate=pl.CostEstimate(
            flops=20 * seq_len * seq_len * local_width,
            bytes_accessed=seq_len * local_width * 14,
            transcendentals=seq_len * seq_len * heads,
        ),
        name="attend_back",
    )(info, qkv, grads, cos_vals, sin_vals)


def gather_rows(own):
    size = lax.axis_size("tp")
    if size == 2:
        return lax.ppermute(own, "tp", [(0, 1), (1, 0)])
    share = own.shape[0]
    whole = lax.all_gather(own, "tp", axis=0, tiled=True)
    start = (lax.axis_index("tp") + 1) * share
    return lax.dynamic_slice_in_dim(
        jnp.concatenate([whole, whole], axis=0), start, (size - 1) * share, 0
    )


def scatter_rows(own_part, send_part):
    size = lax.axis_size("tp")
    if size == 2:
        return own_part + lax.ppermute(send_part, "tp", [(0, 1), (1, 0)]).astype(F32)
    share = own_part.shape[0]
    ring = jnp.concatenate([own_part.astype(BF16), send_part] * 2, axis=0)
    start = (size - lax.axis_index("tp")) * share
    whole = lax.dynamic_slice_in_dim(ring, start, size * share, 0)
    return lax.psum_scatter(whole.astype(F32), "tp", scatter_dimension=0, tiled=True)


def all_sum(value, axes):
    for axis in axes:
        size = lax.axis_size(axis)
        step = 1
        while step < size:
            value = value + lax.ppermute(value, axis, [(i, i ^ step) for i in range(size)])
            step *= 2
    return value


CORE_SWAP = [(0, 1), (1, 0), (2, 3), (3, 2)]
X_SWAP = [(0, 2), (2, 0), (1, 3), (3, 1)]
Z_NEAR = [(0, 1), (1, 0), (2, 3), (3, 2)]
Z_FAR = [(0, 2), (2, 0), (1, 3), (3, 1)]
GROUP = ("dp", "obj")
tie = lax.optimization_barrier


def columns(array, index, count=4):
    width = array.shape[-1] // count
    return lax.dynamic_slice_in_dim(array, index * width, width, array.ndim - 1)


def give_quarters(make):
    dp_index = lax.axis_index("dp")
    return make(3 - dp_index).astype(BF16), make(dp_index ^ 1).astype(BF16)


def core_stage(make, gives):
    dp_index = lax.axis_index("dp")
    got_far = lax.ppermute(gives[0], "dp", CORE_SWAP)
    got_near = lax.ppermute(gives[1], "dp", CORE_SWAP)
    far = (make(dp_index ^ 2) + got_far.astype(F32)).astype(BF16)
    return far, make(dp_index) + got_near.astype(F32)


def x_stage(far, near):
    return near + lax.ppermute(far, "dp", X_SWAP).astype(F32)


def z_near_stage(near, axis):
    obj_index = lax.axis_index("obj")
    width = near.shape[axis] // lax.axis_size("obj")

    def pieces(first):
        return jnp.stack(
            [
                lax.dynamic_slice_in_dim(near, index * width, width, axis)
                for index in (first, first ^ 2)
            ]
        )

    got = lax.ppermute(pieces(obj_index ^ 1).astype(BF16), "obj", Z_NEAR)
    return pieces(obj_index) + got.astype(F32)


def z_far_stage(pair):
    got = lax.ppermute(pair[1].astype(BF16), "obj", Z_FAR)
    return (pair[0] + got.astype(F32)).astype(BF16)


def gather_rows_of(share):
    return lax.all_gather(share, GROUP, axis=0, tiled=True)


def gather_columns_of(share):
    return lax.all_gather(share, GROUP, axis=0, tiled=False)


def widen(stacked):
    return jnp.concatenate([stacked[i] for i in range(stacked.shape[0])], axis=1).astype(F32)


def token_sum(left, right):
    return lax.dot_general(left, right, (((0,), (0,)), ((), ())), preferred_element_type=F32)


def norm_stats(rows):
    mean = jnp.mean(rows, axis=-1, keepdims=True)
    centred = rows - mean
    scale = lax.rsqrt(jnp.mean(centred * centred, axis=-1, keepdims=True) + NORM_EPS)
    return centred * scale, scale


def norm_back(grads, zhat, scale, gain):
    q = grads * gain
    d_rows = scale * (
        q - jnp.mean(q, axis=-1, keepdims=True) - zhat * jnp.mean(q * zhat, axis=-1, keepdims=True)
    )
    return d_rows, jnp.sum(grads * zhat, axis=0), jnp.sum(grads, axis=0)


def body(
    hidden_in,
    cotangent,
    loss_mask,
    prefix_len,
    w_qkv,
    w_out,
    gain_one,
    bias_one,
    w_gate_up,
    w_down,
    gain_two,
    bias_two,
):
    tp_index = lax.axis_index("tp")
    share_len, width = hidden_in.shape[1:]
    seq_len = share_len * lax.axis_size("tp")
    local_ff = w_down.shape[0]
    mask_vals = loss_mask[0].astype(F32)
    total_count = all_sum(jnp.full((8, 128), jnp.sum(mask_vals)), ("dp", "tp"))[0, 0]

    positions = (tp_index * share_len + jnp.arange(seq_len, dtype=jnp.int32)) % seq_len
    half = HEAD_DIM // 2
    frequency = 10000.0 ** (-jnp.arange(half).astype(F32) / half)
    angles = positions.astype(F32)[:, None] * frequency[None, :]
    cos_half, sin_half = jnp.cos(angles), jnp.sin(angles)
    cos_vals = jnp.concatenate([cos_half, cos_half], axis=1)
    sin_vals = jnp.concatenate([-sin_half, sin_half], axis=1)
    info = jnp.stack([tp_index * share_len, prefix_len[0]]).astype(jnp.int32)

    def project(rows):
        return jnp.einsum("td,dke->kte", rows, w_qkv, preferred_element_type=F32)

    x_own = hidden_in[0]
    x_other = gather_rows(x_own)
    mixed, qkv = attend(info, project(x_own), project(x_other), cos_vals, sin_vals)
    mixed_own, mixed_other = mixed[:share_len], mixed[share_len:]
    out_send = jnp.dot(mixed_other, w_out, preferred_element_type=F32).astype(BF16)
    out_own = jnp.dot(mixed_own, w_out, preferred_element_type=F32)
    z_one = DEEP_ALPHA * x_own.astype(F32) + scatter_rows(out_own, out_send)
    zhat_one, scale_one = norm_stats(z_one)
    h_one = zhat_one * gain_one + bias_one
    h_own = h_one.astype(BF16)
    h_other = gather_rows(h_own)

    def feed(rows):
        gate_up = jnp.einsum("td,dke->tke", rows, w_gate_up, preferred_element_type=F32)
        gate, up = gate_up[:, 0], gate_up[:, 1]
        phi = 0.5 * (1.0 + lax.erf(gate * (0.5**0.5)))
        density = jnp.exp(-0.5 * gate * gate) * (0.5 / jnp.pi) ** 0.5
        act = gate * phi
        return lax.optimization_barrier(
            ((act * up).astype(BF16), up * (phi + gate * density), act)
        )

    hidden_own, slope_own, act_own = feed(h_own)
    hidden_other, slope_other, act_other = feed(h_other)
    ffn_send = jnp.dot(hidden_other, w_down, preferred_element_type=F32).astype(BF16)
    ffn_own = jnp.dot(hidden_own, w_down, preferred_element_type=F32)
    z_two = DEEP_ALPHA * h_one + scatter_rows(ffn_own, ffn_send)
    zhat_two, scale_two = norm_stats(z_two)
    outputs = (zhat_two * gain_two + bias_two).astype(BF16)
    grad_y = cotangent[0].astype(F32) * (mask_vals * (seq_len / total_count))[:, None]
    d_z_two, d_gain_two, d_bias_two = norm_back(grad_y, zhat_two, scale_two, gain_two)

    d_ffn_own = d_z_two.astype(BF16)
    d_ffn_other = gather_rows(d_ffn_own)
    hidden = jnp.concatenate([hidden_own, hidden_other], axis=0)
    d_ffn = jnp.concatenate([d_ffn_own, d_ffn_other], axis=0)

    def feed_back(d_rows, slope, act):
        d_hidden = lax.dot_general(
            d_rows, w_down, (((1,), (1,)), ((), ())), preferred_element_type=F32
        )
        return jnp.stack([d_hidden * slope, d_hidden * act], axis=0).astype(BF16)

    def make_down(q):
        return token_sum(hidden, columns(d_ffn, q))

    gives_down, d_ffn_own, d_ffn_other = tie((give_quarters(make_down), d_ffn_own, d_ffn_other))
    d_gu_other = feed_back(d_ffn_other, slope_other, act_other)
    (far_down, near_down), d_gu_other = tie((core_stage(make_down, gives_down), d_gu_other))
    near_down = x_stage(far_down, near_down)

    def feed_rows(d_gate_up):
        return jnp.einsum("kte,dke->td", d_gate_up, w_gate_up, preferred_element_type=F32)

    d_h_send = feed_rows(d_gu_other).astype(BF16)
    d_gu_own = feed_back(d_ffn_own, slope_own, act_own)
    d_gu = jnp.concatenate([d_gu_own, d_gu_other], axis=1)
    h_rows = jnp.concatenate([h_own, h_other], axis=0)

    def make_gate(q):
        return token_sum(columns(h_rows, q), d_gu[0])

    def make_up(q):
        return token_sum(columns(h_rows, q), d_gu[1])

    d_h = scatter_rows(feed_rows(d_gu_own), d_h_send)
    d_h, (far_gate, near_gate), near_down = tie(
        (d_h, core_stage(make_gate, give_quarters(make_gate)), near_down)
    )
    pair_down = z_near_stage(near_down, 1)
    near_gate = x_stage(far_gate, near_gate)
    d_z_one, d_gain_one, d_bias_one = norm_back(
        DEEP_ALPHA * d_z_two + d_h, zhat_one, scale_one, gain_one
    )
    d_attn_own = d_z_one.astype(BF16)
    d_attn_other = gather_rows(d_attn_own)
    d_attn_other, (far_up, near_up), near_gate, pair_down = tie(
        (d_attn_other, core_stage(make_up, give_quarters(make_up)), near_gate, pair_down)
    )
    near_up = x_stage(far_up, near_up)
    pair_gate = z_near_stage(near_gate, 0)
    share_down = z_far_stage(pair_down)
    d_attn = jnp.concatenate([d_attn_own, d_attn_other], axis=0)

    def make_out(q):
        return token_sum(columns(d_attn, q), mixed)

    gives_out, d_attn_own, d_attn_other = tie((give_quarters(make_out), d_attn_own, d_attn_other))

    def unmix(d_rows):
        return lax.dot_general(
            d_rows, w_out, (((1,), (1,)), ((), ())), preferred_element_type=F32
        ).astype(BF16)

    d_mixed = jnp.concatenate([unmix(d_attn_own), unmix(d_attn_other)], axis=0)
    d_mixed, (far_out, near_out), share_down = tie(
        (d_mixed, core_stage(make_out, gives_out), share_down)
    )
    near_out = x_stage(far_out, near_out)
    all_down = gather_columns_of(share_down)
    d_qkv = attend_back(info, qkv, d_mixed, cos_vals, sin_vals)
    d_qkv, near_up, pair_gate = tie((d_qkv, near_up, pair_gate))
    pair_up = z_near_stage(near_up, 0)
    share_gate = z_far_stage(pair_gate)
    x_rows = jnp.concatenate([x_own, x_other], axis=0)

    def make_qkv(k):
        return lambda q: token_sum(columns(x_rows, q), d_qkv[k])

    gives_qkv = [give_quarters(make_qkv(k)) for k in range(3)]

    def unproject(d_rows):
        return jnp.einsum("kte,dke->td", d_rows, w_qkv, preferred_element_type=F32)

    parts_qkv = [core_stage(make_qkv(k), gives_qkv[k]) for k in range(3)]
    parts_qkv, near_out = tie((parts_qkv, near_out))
    pair_out = z_near_stage(near_out, 0)
    near_qkv = [x_stage(far, near) for far, near in parts_qkv]
    d_x_send = unproject(d_qkv[:, share_len:]).astype(BF16)
    d_x_send, pair_up, share_gate = tie((d_x_send, pair_up, share_gate))
    share_up = z_far_stage(pair_up)
    share_out = z_far_stage(pair_out)
    all_gate = gather_rows_of(share_gate)
    near_qkv, share_up, share_out, all_down = tie((near_qkv, share_up, share_out, all_down))
    d_x = scatter_rows(unproject(d_qkv[:, :share_len]), d_x_send)
    input_grad = DEEP_ALPHA * d_z_one + d_x

    norm_terms = all_sum(
        jnp.stack([d_gain_one, d_bias_one, d_gain_two, d_bias_two]), ("dp", "obj", "tp")
    )
    local = width // lax.axis_size("tp")
    norm_terms = lax.dynamic_slice_in_dim(norm_terms, tp_index * local, local, 1)

    all_up_out = gather_rows_of(jnp.concatenate([share_up, share_out], axis=1))
    share_qkv = [z_far_stage(z_near_stage(near, 0)) for near in near_qkv]
    share_qkv, all_gate, all_up_out = tie((share_qkv, all_gate, all_up_out))
    grad_qkv = gather_rows_of(jnp.stack(share_qkv, axis=1)).astype(F32)
    all_up, all_out = all_up_out[:, :local_ff], all_up_out[:, local_ff:]
    grad_gate_up = tie(jnp.stack([all_gate, all_up], axis=1)).astype(F32)
    grad_down = widen(all_down)
    grad_out = all_out.T.astype(F32)
    return (
        outputs[None],
        input_grad[None],
        grad_qkv,
        grad_out,
        norm_terms[0],
        norm_terms[1],
        grad_gate_up,
        grad_down,
        norm_terms[2],
        norm_terms[3],
    )


def solution(mesh):
    return jax.shard_map(
        body,
        mesh=mesh,
        in_specs=(
            P(("obj", "dp"), "tp", None),
            P(("obj", "dp"), "tp", None),
            P(("obj", "dp"), "tp"),
            P(("obj", "dp")),
            P(None, None, "tp"),
            P("tp", None),
            P(),
            P(),
            P(None, None, "tp"),
            P("tp", None),
            P(),
            P(),
        ),
        out_specs=(
            P(("obj", "dp"), "tp", None),
            P(("obj", "dp"), "tp", None),
            P(None, None, "tp"),
            P("tp", None),
            P("tp"),
            P("tp"),
            P(None, None, "tp"),
            P("tp", None),
            P("tp"),
            P("tp"),
        ),
        check_vma=False,
    )
```

```python
import functools

import jax
import jax.numpy as jnp
from jax import lax
from jax.experimental import pallas as pl
from jax.experimental.pallas import tpu as pltpu
from jax.sharding import PartitionSpec as P

HEAD_DIM = 128
DEEP_ALPHA = 48.0**0.5
NORM_EPS = 1e-05
MASKED_SCORE = -1e30
F32 = jnp.float32
BF16 = jnp.bfloat16
VMEM_BYTES = 60 * 1024 * 1024


def rotated(block, cos_ref, sin_ref, sign):
    half = block.shape[-1] // 2
    return block * cos_ref[...] + sign * (pltpu.roll(block, half, 1) * sin_ref[...])


def row_limits(info_ref, start, rows, seq_len):
    row_ids = lax.broadcasted_iota(jnp.int32, (1, rows), 1) + start + info_ref[0]
    row_ids = jnp.where(row_ids >= seq_len, row_ids - seq_len, row_ids)
    return jnp.maximum(row_ids, info_ref[1] - 1)


def key_ids(info_ref, seq_len):
    ids = lax.broadcasted_iota(jnp.int32, (seq_len, 1), 0) + info_ref[0]
    return jnp.where(ids >= seq_len, ids - seq_len, ids)


def attend_kernel(
    block_rows, info_ref, own_ref, other_ref, cos_ref, sin_ref, mixed_ref, qkv_ref
):
    share_len = own_ref.shape[1]
    seq_len = mixed_ref.shape[0]
    scale = HEAD_DIM**-0.5
    for part in range(3):
        block = jnp.concatenate([own_ref[part], other_ref[part]], axis=0)
        if part < 2:
            block = rotated(block, cos_ref, sin_ref, 1.0)
        qkv_ref[part] = block.astype(BF16)
    keys = qkv_ref[1]
    values = qkv_ref[2]
    ids = key_ids(info_ref, seq_len)
    for start in range(0, seq_len, block_rows):
        queries = qkv_ref[0, start : start + block_rows, :]
        scores = (
            lax.dot_general(keys, queries, (((1,), (1,)), ((), ())), preferred_element_type=F32)
            * scale
        )
        limits = row_limits(info_ref, start, block_rows, seq_len)
        scores = jnp.where(ids <= limits, scores, MASKED_SCORE)
        row_max = jnp.max(scores, axis=0, keepdims=True)
        weights = jnp.exp(scores - row_max)
        total = jnp.sum(weights, axis=0, keepdims=True)
        probs = (weights * (1.0 / total)).astype(BF16)
        mixed = lax.dot_general(
            probs, values, (((0,), (0,)), ((), ())), preferred_element_type=F32
        )
        mixed_ref[start : start + block_rows, :] = mixed.astype(BF16)


def attend_back_kernel(
    block_rows, info_ref, qkv_ref, grad_ref, cos_ref, sin_ref, out_ref, d_key_ref, d_value_ref
):
    seq_len = grad_ref.shape[0]
    scale = HEAD_DIM**-0.5
    keys = qkv_ref[1]
    values = qkv_ref[2]
    ids = key_ids(info_ref, seq_len)
    for start in range(0, seq_len, block_rows):
        rows = slice(start, start + block_rows)
        queries = qkv_ref[0, rows, :]
        grads = grad_ref[rows, :]
        scores = (
            lax.dot_general(keys, queries, (((1,), (1,)), ((), ())), preferred_element_type=F32)
            * scale
        )
        limits = row_limits(info_ref, start, block_rows, seq_len)
        scores = jnp.where(ids <= limits, scores, MASKED_SCORE)
        row_max = jnp.max(scores, axis=0, keepdims=True)
        weights = jnp.exp(scores - row_max)
        total = jnp.sum(weights, axis=0, keepdims=True)
        probs = weights * (1.0 / total)
        d_probs = lax.dot_general(
            values, grads, (((1,), (1,)), ((), ())), preferred_element_type=F32
        )
        delta = jnp.sum(probs * d_probs, axis=0, keepdims=True)
        d_scores = (probs * (d_probs - delta)).astype(BF16)
        d_value = jnp.dot(probs.astype(BF16), grads, preferred_element_type=F32)
        d_key = jnp.dot(d_scores, queries, preferred_element_type=F32)
        if start == 0:
            d_value_ref[...] = d_value
            d_key_ref[...] = d_key
        else:
            d_value_ref[...] += d_value
            d_key_ref[...] += d_key
        d_query = (
            lax.dot_general(d_scores, keys, (((0,), (0,)), ((), ())), preferred_element_type=F32)
            * scale
        )
        d_query = d_query * cos_ref[rows, :] - (
            pltpu.roll(d_query, HEAD_DIM // 2, 1) * sin_ref[rows, :]
        )
        out_ref[0, rows, :] = d_query.astype(BF16)
    d_key = d_key_ref[...] * scale
    out_ref[1] = rotated(d_key, cos_ref, sin_ref, -1.0).astype(BF16)
    out_ref[2] = d_value_ref[...].astype(BF16)


def attend(info, own, other, cos_vals, sin_vals):
    share_len, local_width = own.shape[1:]
    seq_len = share_len + other.shape[1]
    heads = local_width // HEAD_DIM
    table = pl.BlockSpec((seq_len, HEAD_DIM), lambda h, info: (0, 0))
    return pl.pallas_call(
        functools.partial(attend_kernel, min(256, seq_len)),
        grid_spec=pltpu.PrefetchScalarGridSpec(
            num_scalar_prefetch=1,
            grid=(heads,),
            in_specs=[
                pl.BlockSpec((3, share_len, HEAD_DIM), lambda h, info: (0, 0, h)),
                pl.BlockSpec((3, seq_len - share_len, HEAD_DIM), lambda h, info: (0, 0, h)),
                table,
                table,
            ],
            out_specs=[
                pl.BlockSpec((seq_len, HEAD_DIM), lambda h, info: (0, h)),
                pl.BlockSpec((3, seq_len, HEAD_DIM), lambda h, info: (0, 0, h)),
            ],
        ),
        out_shape=[
            jax.ShapeDtypeStruct((seq_len, local_width), BF16),
            jax.ShapeDtypeStruct((3, seq_len, local_width), BF16),
        ],
        compiler_params=pltpu.CompilerParams(vmem_limit_bytes=VMEM_BYTES),
        cost_estimate=pl.CostEstimate(
            flops=8 * seq_len * seq_len * local_width,
            bytes_accessed=seq_len * local_width * 20,
            transcendentals=seq_len * seq_len * heads,
        ),
        name="attend",
    )(info, own, other, cos_vals, sin_vals)


def attend_back(info, qkv, grads, cos_vals, sin_vals):
    seq_len, local_width = grads.shape
    heads = local_width // HEAD_DIM
    table = pl.BlockSpec((seq_len, HEAD_DIM), lambda h, info: (0, 0))
    return pl.pallas_call(
        functools.partial(attend_back_kernel, min(256, seq_len)),
        grid_spec=pltpu.PrefetchScalarGridSpec(
            num_scalar_prefetch=1,
            grid=(heads,),
            in_specs=[
                pl.BlockSpec((3, seq_len, HEAD_DIM), lambda h, info: (0, 0, h)),
                pl.BlockSpec((seq_len, HEAD_DIM), lambda h, info: (0, h)),
                table,
                table,
            ],
            out_specs=pl.BlockSpec((3, seq_len, HEAD_DIM), lambda h, info: (0, 0, h)),
            scratch_shapes=[
                pltpu.VMEM((seq_len, HEAD_DIM), F32),
                pltpu.VMEM((seq_len, HEAD_DIM), F32),
            ],
        ),
        out_shape=jax.ShapeDtypeStruct((3, seq_len, local_width), BF16),
        compiler_params=pltpu.CompilerParams(vmem_limit_bytes=VMEM_BYTES),
        cost_estimate=pl.CostEstimate(
            flops=20 * seq_len * seq_len * local_width,
            bytes_accessed=seq_len * local_width * 14,
            transcendentals=seq_len * seq_len * heads,
        ),
        name="attend_back",
    )(info, qkv, grads, cos_vals, sin_vals)


def gather_rows(own):
    size = lax.axis_size("tp")
    if size == 2:
        return lax.ppermute(own, "tp", [(0, 1), (1, 0)])
    share = own.shape[0]
    whole = lax.all_gather(own, "tp", axis=0, tiled=True)
    start = (lax.axis_index("tp") + 1) * share
    return lax.dynamic_slice_in_dim(
        jnp.concatenate([whole, whole], axis=0), start, (size - 1) * share, 0
    )


def scatter_rows(own_part, send_part):
    size = lax.axis_size("tp")
    if size == 2:
        return own_part + lax.ppermute(send_part, "tp", [(0, 1), (1, 0)]).astype(F32)
    share = own_part.shape[0]
    ring = jnp.concatenate([own_part.astype(BF16), send_part] * 2, axis=0)
    start = (size - lax.axis_index("tp")) * share
    whole = lax.dynamic_slice_in_dim(ring, start, size * share, 0)
    return lax.psum_scatter(whole.astype(F32), "tp", scatter_dimension=0, tiled=True)


def all_sum(value, axes):
    for axis in axes:
        size = lax.axis_size(axis)
        step = 1
        while step < size:
            value = value + lax.ppermute(value, axis, [(i, i ^ step) for i in range(size)])
            step *= 2
    return value


CORE_SWAP = [(0, 1), (1, 0), (2, 3), (3, 2)]
X_SWAP = [(0, 2), (2, 0), (1, 3), (3, 1)]
Z_NEAR = [(0, 1), (1, 0), (2, 3), (3, 2)]
Z_FAR = [(0, 2), (2, 0), (1, 3), (3, 1)]
GROUP = ("dp", "obj")
tie = lax.optimization_barrier


def columns(array, index, count=4):
    width = array.shape[-1] // count
    return lax.dynamic_slice_in_dim(array, index * width, width, array.ndim - 1)


def give_quarters(make):
    dp_index = lax.axis_index("dp")
    return make(3 - dp_index).astype(BF16), make(dp_index ^ 1).astype(BF16)


def core_stage(make, gives):
    dp_index = lax.axis_index("dp")
    got_far = lax.ppermute(gives[0], "dp", CORE_SWAP)
    got_near = lax.ppermute(gives[1], "dp", CORE_SWAP)
    far = (make(dp_index ^ 2) + got_far.astype(F32)).astype(BF16)
    return far, make(dp_index) + got_near.astype(F32)


def x_stage(far, near):
    return near + lax.ppermute(far, "dp", X_SWAP).astype(F32)


def z_near_stage(near, axis):
    obj_index = lax.axis_index("obj")
    width = near.shape[axis] // lax.axis_size("obj")

    def pieces(first):
        return jnp.stack(
            [
                lax.dynamic_slice_in_dim(near, index * width, width, axis)
                for index in (first, first ^ 2)
            ]
        )

    got = lax.ppermute(pieces(obj_index ^ 1).astype(BF16), "obj", Z_NEAR)
    return pieces(obj_index) + got.astype(F32)


def z_far_stage(pair):
    got = lax.ppermute(pair[1].astype(BF16), "obj", Z_FAR)
    return (pair[0] + got.astype(F32)).astype(BF16)


def gather_rows_of(share):
    return lax.all_gather(share, GROUP, axis=0, tiled=True)


def gather_columns_of(share):
    return lax.all_gather(share, GROUP, axis=0, tiled=False)


def widen(stacked):
    return jnp.concatenate([stacked[i] for i in range(stacked.shape[0])], axis=1).astype(F32)


def token_sum(left, right):
    return lax.dot_general(left, right, (((0,), (0,)), ((), ())), preferred_element_type=F32)


def norm_stats(rows):
    mean = jnp.mean(rows, axis=-1, keepdims=True)
    centred = rows - mean
    scale = lax.rsqrt(jnp.mean(centred * centred, axis=-1, keepdims=True) + NORM_EPS)
    return centred * scale, scale


def norm_back(grads, zhat, scale, gain):
    q = grads * gain
    d_rows = scale * (
        q - jnp.mean(q, axis=-1, keepdims=True) - zhat * jnp.mean(q * zhat, axis=-1, keepdims=True)
    )
    return d_rows, jnp.sum(grads * zhat, axis=0), jnp.sum(grads, axis=0)


def body(
    hidden_in,
    cotangent,
    loss_mask,
    prefix_len,
    w_qkv,
    w_out,
    gain_one,
    bias_one,
    w_gate_up,
    w_down,
    gain_two,
    bias_two,
):
    tp_index = lax.axis_index("tp")
    share_len, width = hidden_in.shape[1:]
    seq_len = share_len * lax.axis_size("tp")
    local_ff = w_down.shape[0]
    mask_vals = loss_mask[0].astype(F32)
    total_count = all_sum(jnp.full((8, 128), jnp.sum(mask_vals)), ("dp", "tp"))[0, 0]

    positions = (tp_index * share_len + jnp.arange(seq_len, dtype=jnp.int32)) % seq_len
    half = HEAD_DIM // 2
    frequency = 10000.0 ** (-jnp.arange(half).astype(F32) / half)
    angles = positions.astype(F32)[:, None] * frequency[None, :]
    cos_half, sin_half = jnp.cos(angles), jnp.sin(angles)
    cos_vals = jnp.concatenate([cos_half, cos_half], axis=1)
    sin_vals = jnp.concatenate([-sin_half, sin_half], axis=1)
    info = jnp.stack([tp_index * share_len, prefix_len[0]]).astype(jnp.int32)

    def project(rows):
        return jnp.einsum("td,dke->kte", rows, w_qkv, preferred_element_type=F32)

    x_own = hidden_in[0]
    x_other = gather_rows(x_own)
    mixed, qkv = attend(info, project(x_own), project(x_other), cos_vals, sin_vals)
    mixed_own, mixed_other = mixed[:share_len], mixed[share_len:]
    out_send = jnp.dot(mixed_other, w_out, preferred_element_type=F32).astype(BF16)
    out_own = jnp.dot(mixed_own, w_out, preferred_element_type=F32)
    z_one = DEEP_ALPHA * x_own.astype(F32) + scatter_rows(out_own, out_send)
    zhat_one, scale_one = norm_stats(z_one)
    h_one = zhat_one * gain_one + bias_one
    h_own = h_one.astype(BF16)
    h_other = gather_rows(h_own)

    def feed(rows):
        gate_up = jnp.einsum("td,dke->tke", rows, w_gate_up, preferred_element_type=F32)
        gate, up = gate_up[:, 0], gate_up[:, 1]
        phi = 0.5 * (1.0 + lax.erf(gate * (0.5**0.5)))
        density = jnp.exp(-0.5 * gate * gate) * (0.5 / jnp.pi) ** 0.5
        act = gate * phi
        return lax.optimization_barrier(
            ((act * up).astype(BF16), up * (phi + gate * density), act)
        )

    hidden_own, slope_own, act_own = feed(h_own)
    hidden_other, slope_other, act_other = feed(h_other)
    ffn_send = jnp.dot(hidden_other, w_down, preferred_element_type=F32).astype(BF16)
    ffn_own = jnp.dot(hidden_own, w_down, preferred_element_type=F32)
    z_two = DEEP_ALPHA * h_one + scatter_rows(ffn_own, ffn_send)
    zhat_two, scale_two = norm_stats(z_two)
    outputs = (zhat_two * gain_two + bias_two).astype(BF16)
    grad_y = cotangent[0].astype(F32) * (mask_vals * (seq_len / total_count))[:, None]
    d_z_two, d_gain_two, d_bias_two = norm_back(grad_y, zhat_two, scale_two, gain_two)

    d_ffn_own = d_z_two.astype(BF16)
    d_ffn_other = gather_rows(d_ffn_own)
    hidden = jnp.concatenate([hidden_own, hidden_other], axis=0)
    d_ffn = jnp.concatenate([d_ffn_own, d_ffn_other], axis=0)

    def feed_back(d_rows, slope, act):
        d_hidden = lax.dot_general(
            d_rows, w_down, (((1,), (1,)), ((), ())), preferred_element_type=F32
        )
        return jnp.stack([d_hidden * slope, d_hidden * act], axis=0).astype(BF16)

    def make_down(q):
        return token_sum(hidden, columns(d_ffn, q))

    gives_down, d_ffn_own, d_ffn_other = tie((give_quarters(make_down), d_ffn_own, d_ffn_other))
    d_gu_other = feed_back(d_ffn_other, slope_other, act_other)
    (far_down, near_down), d_gu_other = tie((core_stage(make_down, gives_down), d_gu_other))
    near_down = x_stage(far_down, near_down)

    def feed_rows(d_gate_up):
        return jnp.einsum("kte,dke->td", d_gate_up, w_gate_up, preferred_element_type=F32)

    d_h_send = feed_rows(d_gu_other).astype(BF16)
    d_gu_own = feed_back(d_ffn_own, slope_own, act_own)
    d_gu = jnp.concatenate([d_gu_own, d_gu_other], axis=1)
    h_rows = jnp.concatenate([h_own, h_other], axis=0)

    def make_gate(q):
        return token_sum(columns(h_rows, q), d_gu[0])

    def make_up(q):
        return token_sum(columns(h_rows, q), d_gu[1])

    d_h = scatter_rows(feed_rows(d_gu_own), d_h_send)
    d_h, (far_gate, near_gate), near_down = tie(
        (d_h, core_stage(make_gate, give_quarters(make_gate)), near_down)
    )
    pair_down = z_near_stage(near_down, 1)
    near_gate = x_stage(far_gate, near_gate)
    d_z_one, d_gain_one, d_bias_one = norm_back(
        DEEP_ALPHA * d_z_two + d_h, zhat_one, scale_one, gain_one
    )
    d_attn_own = d_z_one.astype(BF16)
    d_attn_other = gather_rows(d_attn_own)
    d_attn_other, (far_up, near_up), near_gate, pair_down = tie(
        (d_attn_other, core_stage(make_up, give_quarters(make_up)), near_gate, pair_down)
    )
    near_up = x_stage(far_up, near_up)
    pair_gate = z_near_stage(near_gate, 0)
    share_down = z_far_stage(pair_down)
    d_attn = jnp.concatenate([d_attn_own, d_attn_other], axis=0)

    def make_out(q):
        return token_sum(columns(d_attn, q), mixed)

    gives_out, d_attn_own, d_attn_other = tie((give_quarters(make_out), d_attn_own, d_attn_other))

    def unmix(d_rows):
        return lax.dot_general(
            d_rows, w_out, (((1,), (1,)), ((), ())), preferred_element_type=F32
        ).astype(BF16)

    d_mixed = jnp.concatenate([unmix(d_attn_own), unmix(d_attn_other)], axis=0)
    d_mixed, (far_out, near_out) = tie((d_mixed, core_stage(make_out, gives_out)))
    near_out = x_stage(far_out, near_out)
    d_qkv = attend_back(info, qkv, d_mixed, cos_vals, sin_vals)
    d_qkv, near_up, pair_gate, share_down = tie((d_qkv, near_up, pair_gate, share_down))
    all_down = gather_columns_of(share_down)
    pair_up = z_near_stage(near_up, 0)
    share_gate = z_far_stage(pair_gate)
    x_rows = jnp.concatenate([x_own, x_other], axis=0)

    def make_qkv(k):
        return lambda q: token_sum(columns(x_rows, q), d_qkv[k])

    gives_qkv = [give_quarters(make_qkv(k)) for k in range(3)]

    def unproject(d_rows):
        return jnp.einsum("kte,dke->td", d_rows, w_qkv, preferred_element_type=F32)

    parts_qkv = [core_stage(make_qkv(k), gives_qkv[k]) for k in range(3)]
    parts_qkv, near_out, pair_up = tie((parts_qkv, near_out, pair_up))
    pair_out = z_near_stage(near_out, 0)
    near_qkv = [x_stage(far, near) for far, near in parts_qkv]
    d_x_send = unproject(d_qkv[:, share_len:]).astype(BF16)
    share_up = z_far_stage(pair_up)
    share_out = z_far_stage(pair_out)
    near_qkv, share_gate, share_up, share_out, all_down = tie(
        (near_qkv, share_gate, share_up, share_out, all_down)
    )
    d_x = scatter_rows(unproject(d_qkv[:, :share_len]), d_x_send)
    input_grad = DEEP_ALPHA * d_z_one + d_x

    norm_terms = all_sum(
        jnp.stack([d_gain_one, d_bias_one, d_gain_two, d_bias_two]), ("dp", "obj", "tp")
    )
    local = width // lax.axis_size("tp")
    norm_terms = lax.dynamic_slice_in_dim(norm_terms, tp_index * local, local, 1)

    all_gate_up = gather_rows_of(jnp.stack([share_gate, share_up], axis=1))
    share_last = [z_far_stage(z_near_stage(near, 0)) for near in near_qkv] + [share_out]
    share_last, all_gate_up = tie((share_last, all_gate_up))
    all_last = gather_rows_of(jnp.stack(share_last, axis=1))
    grad_qkv = all_last[:, :3].astype(F32)
    grad_out = all_last[:, 3].T.astype(F32)
    grad_gate_up = all_gate_up.astype(F32)
    grad_down = widen(all_down)
    return (
        outputs[None],
        input_grad[None],
        grad_qkv,
        grad_out,
        norm_terms[0],
        norm_terms[1],
        grad_gate_up,
        grad_down,
        norm_terms[2],
        norm_terms[3],
    )


def solution(mesh):
    return jax.shard_map(
        body,
        mesh=mesh,
        in_specs=(
            P(("obj", "dp"), "tp", None),
            P(("obj", "dp"), "tp", None),
            P(("obj", "dp"), "tp"),
            P(("obj", "dp")),
            P(None, None, "tp"),
            P("tp", None),
            P(),
            P(),
            P(None, None, "tp"),
            P("tp", None),
            P(),
            P(),
        ),
        out_specs=(
            P(("obj", "dp"), "tp", None),
            P(("obj", "dp"), "tp", None),
            P(None, None, "tp"),
            P("tp", None),
            P("tp"),
            P("tp"),
            P(None, None, "tp"),
            P("tp", None),
            P("tp"),
            P("tp"),
        ),
        check_vma=False,
    )
```

```python
import functools

import jax
import jax.numpy as jnp
from jax import lax
from jax.experimental import pallas as pl
from jax.experimental.pallas import tpu as pltpu
from jax.sharding import PartitionSpec as P

HEAD_DIM = 128
DEEP_ALPHA = 48.0**0.5
NORM_EPS = 1e-05
MASKED_SCORE = -1e30
F32 = jnp.float32
BF16 = jnp.bfloat16
VMEM_BYTES = 60 * 1024 * 1024


def rotated(block, cos_ref, sin_ref, sign):
    half = block.shape[-1] // 2
    return block * cos_ref[...] + sign * (pltpu.roll(block, half, 1) * sin_ref[...])


def row_limits(info_ref, start, rows, seq_len):
    row_ids = lax.broadcasted_iota(jnp.int32, (1, rows), 1) + start + info_ref[0]
    row_ids = jnp.where(row_ids >= seq_len, row_ids - seq_len, row_ids)
    return jnp.maximum(row_ids, info_ref[1] - 1)


def key_ids(info_ref, seq_len):
    ids = lax.broadcasted_iota(jnp.int32, (seq_len, 1), 0) + info_ref[0]
    return jnp.where(ids >= seq_len, ids - seq_len, ids)


def attend_kernel(
    block_rows, info_ref, own_ref, other_ref, cos_ref, sin_ref, mixed_ref, qkv_ref
):
    share_len = own_ref.shape[1]
    seq_len = mixed_ref.shape[0]
    scale = HEAD_DIM**-0.5
    for part in range(3):
        block = jnp.concatenate([own_ref[part], other_ref[part]], axis=0)
        if part < 2:
            block = rotated(block, cos_ref, sin_ref, 1.0)
        qkv_ref[part] = block.astype(BF16)
    keys = qkv_ref[1]
    values = qkv_ref[2]
    ids = key_ids(info_ref, seq_len)
    for start in range(0, seq_len, block_rows):
        queries = qkv_ref[0, start : start + block_rows, :]
        scores = (
            lax.dot_general(keys, queries, (((1,), (1,)), ((), ())), preferred_element_type=F32)
            * scale
        )
        limits = row_limits(info_ref, start, block_rows, seq_len)
        scores = jnp.where(ids <= limits, scores, MASKED_SCORE)
        row_max = jnp.max(scores, axis=0, keepdims=True)
        weights = jnp.exp(scores - row_max)
        total = jnp.sum(weights, axis=0, keepdims=True)
        probs = (weights * (1.0 / total)).astype(BF16)
        mixed = lax.dot_general(
            probs, values, (((0,), (0,)), ((), ())), preferred_element_type=F32
        )
        mixed_ref[start : start + block_rows, :] = mixed.astype(BF16)


def attend_back_kernel(
    block_rows, info_ref, qkv_ref, grad_ref, cos_ref, sin_ref, out_ref, d_key_ref, d_value_ref
):
    seq_len = grad_ref.shape[0]
    scale = HEAD_DIM**-0.5
    keys = qkv_ref[1]
    values = qkv_ref[2]
    ids = key_ids(info_ref, seq_len)
    for start in range(0, seq_len, block_rows):
        rows = slice(start, start + block_rows)
        queries = qkv_ref[0, rows, :]
        grads = grad_ref[rows, :]
        scores = (
            lax.dot_general(keys, queries, (((1,), (1,)), ((), ())), preferred_element_type=F32)
            * scale
        )
        limits = row_limits(info_ref, start, block_rows, seq_len)
        scores = jnp.where(ids <= limits, scores, MASKED_SCORE)
        row_max = jnp.max(scores, axis=0, keepdims=True)
        weights = jnp.exp(scores - row_max)
        total = jnp.sum(weights, axis=0, keepdims=True)
        probs = weights * (1.0 / total)
        d_probs = lax.dot_general(
            values, grads, (((1,), (1,)), ((), ())), preferred_element_type=F32
        )
        delta = jnp.sum(probs * d_probs, axis=0, keepdims=True)
        d_scores = (probs * (d_probs - delta)).astype(BF16)
        d_value = jnp.dot(probs.astype(BF16), grads, preferred_element_type=F32)
        d_key = jnp.dot(d_scores, queries, preferred_element_type=F32)
        if start == 0:
            d_value_ref[...] = d_value
            d_key_ref[...] = d_key
        else:
            d_value_ref[...] += d_value
            d_key_ref[...] += d_key
        d_query = (
            lax.dot_general(d_scores, keys, (((0,), (0,)), ((), ())), preferred_element_type=F32)
            * scale
        )
        d_query = d_query * cos_ref[rows, :] - (
            pltpu.roll(d_query, HEAD_DIM // 2, 1) * sin_ref[rows, :]
        )
        out_ref[0, rows, :] = d_query.astype(BF16)
    d_key = d_key_ref[...] * scale
    out_ref[1] = rotated(d_key, cos_ref, sin_ref, -1.0).astype(BF16)
    out_ref[2] = d_value_ref[...].astype(BF16)


def attend(info, own, other, cos_vals, sin_vals):
    share_len, local_width = own.shape[1:]
    seq_len = share_len + other.shape[1]
    heads = local_width // HEAD_DIM
    table = pl.BlockSpec((seq_len, HEAD_DIM), lambda h, info: (0, 0))
    return pl.pallas_call(
        functools.partial(attend_kernel, min(256, seq_len)),
        grid_spec=pltpu.PrefetchScalarGridSpec(
            num_scalar_prefetch=1,
            grid=(heads,),
            in_specs=[
                pl.BlockSpec((3, share_len, HEAD_DIM), lambda h, info: (0, 0, h)),
                pl.BlockSpec((3, seq_len - share_len, HEAD_DIM), lambda h, info: (0, 0, h)),
                table,
                table,
            ],
            out_specs=[
                pl.BlockSpec((seq_len, HEAD_DIM), lambda h, info: (0, h)),
                pl.BlockSpec((3, seq_len, HEAD_DIM), lambda h, info: (0, 0, h)),
            ],
        ),
        out_shape=[
            jax.ShapeDtypeStruct((seq_len, local_width), BF16),
            jax.ShapeDtypeStruct((3, seq_len, local_width), BF16),
        ],
        compiler_params=pltpu.CompilerParams(vmem_limit_bytes=VMEM_BYTES),
        cost_estimate=pl.CostEstimate(
            flops=8 * seq_len * seq_len * local_width,
            bytes_accessed=seq_len * local_width * 20,
            transcendentals=seq_len * seq_len * heads,
        ),
        name="attend",
    )(info, own, other, cos_vals, sin_vals)


def attend_back(info, qkv, grads, cos_vals, sin_vals):
    seq_len, local_width = grads.shape
    heads = local_width // HEAD_DIM
    table = pl.BlockSpec((seq_len, HEAD_DIM), lambda h, info: (0, 0))
    return pl.pallas_call(
        functools.partial(attend_back_kernel, min(256, seq_len)),
        grid_spec=pltpu.PrefetchScalarGridSpec(
            num_scalar_prefetch=1,
            grid=(heads,),
            in_specs=[
                pl.BlockSpec((3, seq_len, HEAD_DIM), lambda h, info: (0, 0, h)),
                pl.BlockSpec((seq_len, HEAD_DIM), lambda h, info: (0, h)),
                table,
                table,
            ],
            out_specs=pl.BlockSpec((3, seq_len, HEAD_DIM), lambda h, info: (0, 0, h)),
            scratch_shapes=[
                pltpu.VMEM((seq_len, HEAD_DIM), F32),
                pltpu.VMEM((seq_len, HEAD_DIM), F32),
            ],
        ),
        out_shape=jax.ShapeDtypeStruct((3, seq_len, local_width), BF16),
        compiler_params=pltpu.CompilerParams(vmem_limit_bytes=VMEM_BYTES),
        cost_estimate=pl.CostEstimate(
            flops=20 * seq_len * seq_len * local_width,
            bytes_accessed=seq_len * local_width * 14,
            transcendentals=seq_len * seq_len * heads,
        ),
        name="attend_back",
    )(info, qkv, grads, cos_vals, sin_vals)


def gather_rows(own):
    size = lax.axis_size("tp")
    if size == 2:
        return lax.ppermute(own, "tp", [(0, 1), (1, 0)])
    share = own.shape[0]
    whole = lax.all_gather(own, "tp", axis=0, tiled=True)
    start = (lax.axis_index("tp") + 1) * share
    return lax.dynamic_slice_in_dim(
        jnp.concatenate([whole, whole], axis=0), start, (size - 1) * share, 0
    )


def scatter_rows(own_part, send_part):
    size = lax.axis_size("tp")
    if size == 2:
        return own_part + lax.ppermute(send_part, "tp", [(0, 1), (1, 0)]).astype(F32)
    share = own_part.shape[0]
    ring = jnp.concatenate([own_part.astype(BF16), send_part] * 2, axis=0)
    start = (size - lax.axis_index("tp")) * share
    whole = lax.dynamic_slice_in_dim(ring, start, size * share, 0)
    return lax.psum_scatter(whole.astype(F32), "tp", scatter_dimension=0, tiled=True)


def all_sum(value, axes):
    for axis in axes:
        size = lax.axis_size(axis)
        step = 1
        while step < size:
            value = value + lax.ppermute(value, axis, [(i, i ^ step) for i in range(size)])
            step *= 2
    return value


CORE_SWAP = [(0, 1), (1, 0), (2, 3), (3, 2)]
X_SWAP = [(0, 2), (2, 0), (1, 3), (3, 1)]
Z_NEAR = [(0, 1), (1, 0), (2, 3), (3, 2)]
Z_FAR = [(0, 2), (2, 0), (1, 3), (3, 1)]
GROUP = ("dp", "obj")
tie = lax.optimization_barrier


def columns(array, index, count=4):
    width = array.shape[-1] // count
    return lax.dynamic_slice_in_dim(array, index * width, width, array.ndim - 1)


def give_quarters(make):
    dp_index = lax.axis_index("dp")
    return make(3 - dp_index).astype(BF16), make(dp_index ^ 1).astype(BF16)


def core_stage(make, gives):
    dp_index = lax.axis_index("dp")
    got_far = lax.ppermute(gives[0], "dp", CORE_SWAP)
    got_near = lax.ppermute(gives[1], "dp", CORE_SWAP)
    far = (make(dp_index ^ 2) + got_far.astype(F32)).astype(BF16)
    return far, make(dp_index) + got_near.astype(F32)


def x_stage(far, near):
    return near + lax.ppermute(far, "dp", X_SWAP).astype(F32)


def z_near_stage(near, axis):
    obj_index = lax.axis_index("obj")
    width = near.shape[axis] // lax.axis_size("obj")

    def pieces(first):
        return jnp.stack(
            [
                lax.dynamic_slice_in_dim(near, index * width, width, axis)
                for index in (first, first ^ 2)
            ]
        )

    got = lax.ppermute(pieces(obj_index ^ 1).astype(BF16), "obj", Z_NEAR)
    return pieces(obj_index) + got.astype(F32)


def z_far_stage(pair):
    got = lax.ppermute(pair[1].astype(BF16), "obj", Z_FAR)
    return (pair[0] + got.astype(F32)).astype(BF16)


def gather_rows_of(share):
    return lax.all_gather(share, GROUP, axis=0, tiled=True)


def gather_columns_of(share):
    return lax.all_gather(share, GROUP, axis=0, tiled=False)


def widen(stacked):
    return jnp.concatenate([stacked[i] for i in range(stacked.shape[0])], axis=1).astype(F32)


def token_sum(left, right):
    return lax.dot_general(left, right, (((0,), (0,)), ((), ())), preferred_element_type=F32)


def norm_stats(rows):
    mean = jnp.mean(rows, axis=-1, keepdims=True)
    centred = rows - mean
    scale = lax.rsqrt(jnp.mean(centred * centred, axis=-1, keepdims=True) + NORM_EPS)
    return centred * scale, scale


def norm_back(grads, zhat, scale, gain):
    q = grads * gain
    d_rows = scale * (
        q - jnp.mean(q, axis=-1, keepdims=True) - zhat * jnp.mean(q * zhat, axis=-1, keepdims=True)
    )
    return d_rows, jnp.sum(grads * zhat, axis=0), jnp.sum(grads, axis=0)


def body(
    hidden_in,
    cotangent,
    loss_mask,
    prefix_len,
    w_qkv,
    w_out,
    gain_one,
    bias_one,
    w_gate_up,
    w_down,
    gain_two,
    bias_two,
):
    tp_index = lax.axis_index("tp")
    share_len, width = hidden_in.shape[1:]
    seq_len = share_len * lax.axis_size("tp")
    local_ff = w_down.shape[0]
    mask_vals = loss_mask[0].astype(F32)
    total_count = all_sum(jnp.full((8, 128), jnp.sum(mask_vals)), ("dp", "tp"))[0, 0]

    positions = (tp_index * share_len + jnp.arange(seq_len, dtype=jnp.int32)) % seq_len
    half = HEAD_DIM // 2
    frequency = 10000.0 ** (-jnp.arange(half).astype(F32) / half)
    angles = positions.astype(F32)[:, None] * frequency[None, :]
    cos_half, sin_half = jnp.cos(angles), jnp.sin(angles)
    cos_vals = jnp.concatenate([cos_half, cos_half], axis=1)
    sin_vals = jnp.concatenate([-sin_half, sin_half], axis=1)
    info = jnp.stack([tp_index * share_len, prefix_len[0]]).astype(jnp.int32)

    def project(rows):
        return jnp.einsum("td,dke->kte", rows, w_qkv, preferred_element_type=F32)

    x_own = hidden_in[0]
    x_other = gather_rows(x_own)
    mixed, qkv = attend(info, project(x_own), project(x_other), cos_vals, sin_vals)
    mixed_own, mixed_other = mixed[:share_len], mixed[share_len:]
    out_send = jnp.dot(mixed_other, w_out, preferred_element_type=F32).astype(BF16)
    out_own = jnp.dot(mixed_own, w_out, preferred_element_type=F32)
    z_one = DEEP_ALPHA * x_own.astype(F32) + scatter_rows(out_own, out_send)
    zhat_one, scale_one = norm_stats(z_one)
    h_one = zhat_one * gain_one + bias_one
    h_own = h_one.astype(BF16)
    h_other = gather_rows(h_own)

    def feed(rows):
        gate_up = jnp.einsum("td,dke->tke", rows, w_gate_up, preferred_element_type=F32)
        gate, up = gate_up[:, 0], gate_up[:, 1]
        phi = 0.5 * (1.0 + lax.erf(gate * (0.5**0.5)))
        density = jnp.exp(-0.5 * gate * gate) * (0.5 / jnp.pi) ** 0.5
        act = gate * phi
        return lax.optimization_barrier(
            ((act * up).astype(BF16), up * (phi + gate * density), act)
        )

    hidden_own, slope_own, act_own = feed(h_own)
    hidden_other, slope_other, act_other = feed(h_other)
    ffn_send = jnp.dot(hidden_other, w_down, preferred_element_type=F32).astype(BF16)
    ffn_own = jnp.dot(hidden_own, w_down, preferred_element_type=F32)
    z_two = DEEP_ALPHA * h_one + scatter_rows(ffn_own, ffn_send)
    zhat_two, scale_two = norm_stats(z_two)
    outputs = (zhat_two * gain_two + bias_two).astype(BF16)
    grad_y = cotangent[0].astype(F32) * (mask_vals * (seq_len / total_count))[:, None]
    d_z_two, d_gain_two, d_bias_two = norm_back(grad_y, zhat_two, scale_two, gain_two)

    d_ffn_own = d_z_two.astype(BF16)
    d_ffn_other = gather_rows(d_ffn_own)
    hidden = jnp.concatenate([hidden_own, hidden_other], axis=0)
    d_ffn = jnp.concatenate([d_ffn_own, d_ffn_other], axis=0)

    def feed_back(d_rows, slope, act):
        d_hidden = lax.dot_general(
            d_rows, w_down, (((1,), (1,)), ((), ())), preferred_element_type=F32
        )
        return jnp.stack([d_hidden * slope, d_hidden * act], axis=0).astype(BF16)

    def make_down(q):
        return token_sum(hidden, columns(d_ffn, q))

    gives_down, d_ffn_own, d_ffn_other = tie((give_quarters(make_down), d_ffn_own, d_ffn_other))
    d_gu_other = feed_back(d_ffn_other, slope_other, act_other)
    (far_down, near_down), d_gu_other = tie((core_stage(make_down, gives_down), d_gu_other))
    near_down = x_stage(far_down, near_down)

    def feed_rows(d_gate_up):
        return jnp.einsum("kte,dke->td", d_gate_up, w_gate_up, preferred_element_type=F32)

    d_h_send = feed_rows(d_gu_other).astype(BF16)
    d_gu_own = feed_back(d_ffn_own, slope_own, act_own)
    d_gu = jnp.concatenate([d_gu_own, d_gu_other], axis=1)
    h_rows = jnp.concatenate([h_own, h_other], axis=0)

    def make_gate(q):
        return token_sum(columns(h_rows, q), d_gu[0])

    def make_up(q):
        return token_sum(columns(h_rows, q), d_gu[1])

    d_h = scatter_rows(feed_rows(d_gu_own), d_h_send)
    d_h, (far_gate, near_gate), near_down = tie(
        (d_h, core_stage(make_gate, give_quarters(make_gate)), near_down)
    )
    pair_down = z_near_stage(near_down, 1)
    near_gate = x_stage(far_gate, near_gate)
    d_z_one, d_gain_one, d_bias_one = norm_back(
        DEEP_ALPHA * d_z_two + d_h, zhat_one, scale_one, gain_one
    )
    d_attn_own = d_z_one.astype(BF16)
    d_attn_other = gather_rows(d_attn_own)
    d_attn_other, (far_up, near_up), near_gate, pair_down = tie(
        (d_attn_other, core_stage(make_up, give_quarters(make_up)), near_gate, pair_down)
    )
    near_up = x_stage(far_up, near_up)
    pair_gate = z_near_stage(near_gate, 0)
    share_down = z_far_stage(pair_down)
    d_attn = jnp.concatenate([d_attn_own, d_attn_other], axis=0)

    def make_out(q):
        return token_sum(columns(d_attn, q), mixed)

    gives_out, d_attn_own, d_attn_other = tie((give_quarters(make_out), d_attn_own, d_attn_other))

    def unmix(d_rows):
        return lax.dot_general(
            d_rows, w_out, (((1,), (1,)), ((), ())), preferred_element_type=F32
        ).astype(BF16)

    d_mixed = jnp.concatenate([unmix(d_attn_own), unmix(d_attn_other)], axis=0)
    d_mixed, (far_out, near_out) = tie((d_mixed, core_stage(make_out, gives_out)))
    near_out = x_stage(far_out, near_out)
    d_qkv = attend_back(info, qkv, d_mixed, cos_vals, sin_vals)
    d_qkv, near_up, pair_gate, share_down = tie((d_qkv, near_up, pair_gate, share_down))
    all_down = gather_columns_of(share_down)
    pair_up = z_near_stage(near_up, 0)
    share_gate = z_far_stage(pair_gate)
    x_rows = jnp.concatenate([x_own, x_other], axis=0)

    def make_qkv(k):
        return lambda q: token_sum(columns(x_rows, q), d_qkv[k])

    gives_qkv = [give_quarters(make_qkv(k)) for k in range(3)]

    def unproject(d_rows):
        return jnp.einsum("kte,dke->td", d_rows, w_qkv, preferred_element_type=F32)

    parts_qkv = [core_stage(make_qkv(k), gives_qkv[k]) for k in range(3)]
    parts_qkv, near_out, pair_up = tie((parts_qkv, near_out, pair_up))
    pair_out = z_near_stage(near_out, 0)
    near_qkv = [x_stage(far, near) for far, near in parts_qkv]
    d_x_send = unproject(d_qkv[:, share_len:]).astype(BF16)
    share_up = z_far_stage(pair_up)
    share_out = z_far_stage(pair_out)
    near_qkv, share_gate, share_up, share_out = tie((near_qkv, share_gate, share_up, share_out))
    d_x = scatter_rows(unproject(d_qkv[:, :share_len]), d_x_send)
    input_grad = DEEP_ALPHA * d_z_one + d_x

    norm_terms = all_sum(
        jnp.stack([d_gain_one, d_bias_one, d_gain_two, d_bias_two]), ("dp", "obj", "tp")
    )
    local = width // lax.axis_size("tp")
    norm_terms = lax.dynamic_slice_in_dim(norm_terms, tp_index * local, local, 1)

    all_gate_up = gather_rows_of(jnp.stack([share_gate, share_up], axis=1))
    share_last = [z_far_stage(z_near_stage(near, 0)) for near in near_qkv] + [share_out]
    share_last, all_down = tie((share_last, all_down))
    all_last = gather_rows_of(jnp.stack(share_last, axis=1))
    grad_qkv = all_last[:, :3].astype(F32)
    grad_out = all_last[:, 3].T.astype(F32)
    grad_gate_up = all_gate_up.astype(F32)
    grad_down = widen(all_down)
    return (
        outputs[None],
        input_grad[None],
        grad_qkv,
        grad_out,
        norm_terms[0],
        norm_terms[1],
        grad_gate_up,
        grad_down,
        norm_terms[2],
        norm_terms[3],
    )


def solution(mesh):
    return jax.shard_map(
        body,
        mesh=mesh,
        in_specs=(
            P(("obj", "dp"), "tp", None),
            P(("obj", "dp"), "tp", None),
            P(("obj", "dp"), "tp"),
            P(("obj", "dp")),
            P(None, None, "tp"),
            P("tp", None),
            P(),
            P(),
            P(None, None, "tp"),
            P("tp", None),
            P(),
            P(),
        ),
        out_specs=(
            P(("obj", "dp"), "tp", None),
            P(("obj", "dp"), "tp", None),
            P(None, None, "tp"),
            P("tp", None),
            P("tp"),
            P("tp"),
            P(None, None, "tp"),
            P("tp", None),
            P("tp"),
            P("tp"),
        ),
        check_vma=False,
    )
```
